32 devices in a mesh: dp: 4 (over z), vocab: 8 (over y, x, core).
Axes of the slice: x: 2, y: 2, z: 4, core: 2. Of those that a mesh axis runs over, the one named last changes fastest.
Arguments:
- hidden: bfloat16 [4096, 4096], P(('dp', 'vocab')), may hold values from -4 to 4
- output_weight: bfloat16 [4096, 8192], P(None, 'vocab'), may hold values from -0.09375 to 0.09375
- owners: int32 [4096, 3], P(('dp', 'vocab')), may hold values from 0 to 7, all different within a row; in each aligned block of 128 rows (0 to 127, 128 to 255, ...) at most 64 rows name the same one
- negatives: int32 [4096, 3, 2], P(('dp', 'vocab')), may hold values from 0 to 7
- negative_mask: int32 [4096, 3, 2], P(('dp', 'vocab')), may hold values 0 or 1
- target_block: int32 [4096], P(('dp', 'vocab')), may hold values from 0 to 7
- target_word: int32 [4096], P(('dp', 'vocab')), may hold values from 0 to 127
- log_norm: bfloat16 [4096], P(('dp', 'vocab')), may hold values from 1 to 2
- cotangent: bfloat16 [4096], P(('dp', 'vocab')), may hold values from 4 to 8
Outputs:
- hidden_grad: bfloat16 [4096, 4096], P(('dp', 'vocab'))
- weight_grad: bfloat16 [4096, 8192], P('dp', 'vocab')
The draws below stay inside these ranges and needn't reach their ends.
Inputs may be any that keep to these rules, and one draw needn't show every extreme that they name: Each row names 3 different owners; among the 128 rows of one device no owner is named by more than 64 rows, and in some device's rows an owner is named by exactly 64.
All inputs are finite; a program needn't handle non-finite values. No bound on the sum of `negative_mask` on one device may be relied on, other than what follows from the above.
Results may differ from the reference program's by a relative error of at most 0.015.
Values may be sent and summed in bfloat16 or wider, within the bound.
A program may use at most 128 MiB of HBM per device.

```python
import math
import jax
import jax.numpy as jnp
import numpy as np
from jax import lax

H = 4096
BLOCK = 128
VIS = 3
PER_OWN = 2
BLK_DEV = 8
TOK_DEV = 128
CAP = 64
GROUP_TOK = 1024
TOKENS = 4096
WORDS = 8192
N_DP = 4
N_VOCAB = 8


def set_ends(values, own_key, low, high):
    longest = values.shape.index(max(values.shape))
    spots = []
    for shift in (0, 1):
        where = [jax.random.randint(jax.random.fold_in(own_key, axis), (), 0, length) for axis, length in enumerate(values.shape)]
        where[longest] = (where[longest] + shift) % values.shape[longest]
        spots.append(tuple(where))
    return values.at[spots[0]].set(low).at[spots[1]].set(high)


def block_scale(rng, dims, cuts, least, largest):
    loudness = 1.0
    for position, parts in cuts:
        heights = jax.random.uniform(jax.random.fold_in(jax.random.fold_in(rng, 6), position), (parts,), jnp.float32, least / len(cuts), largest / len(cuts))
        loudness = loudness * jnp.repeat(jnp.exp(heights), dims[position] // parts).reshape((-1,) + (1,) * (len(dims) - 1 - position))
    return loudness


def assign_block(key, own, number, rows, number_of, top, bound, skew):
    sequence = jax.random.permutation(key, number_of)
    crowded, common = load_shares(number_of, rows * top, bound, skew, True), load_shares(number_of, rows * top, bound, skew, False)
    places = jnp.arange(number_of)

    def named(lengths, turn):
        used = int((lengths > 0).sum())
        fixed = max(1, used // 4)
        shifted = fixed + (places - fixed + turn * (used - fixed)) % max(1, number_of - fixed)
        return jnp.zeros((number_of,), jnp.int32).at[sequence[jnp.where(places < fixed, places, shifted)]].set(jnp.asarray(lengths, jnp.int32))

    lengths = jnp.where(number % 4 == 0, named(crowded, number // 4), named(common, number - number // 4 - 1))
    mixed = jax.random.permutation(jax.random.fold_in(own, 3), number_of)
    giver, taker = mixed[0:number_of // 2 * 2:2], mixed[1:number_of // 2 * 2:2]
    slack = jnp.minimum(lengths[giver] - 1, bound - lengths[taker]) // 2
    slack = jnp.where((giver == sequence[0]) | (taker == sequence[0]) | (lengths[taker] == 0), 0, jnp.maximum(slack, 0))
    shifted = jax.random.randint(jax.random.fold_in(own, 4), (number_of // 2,), 0, 1 << 20) % (slack + 1)
    lengths = lengths.at[giver].add(-shifted).at[taker].add(shifted)
    items = jnp.searchsorted(jnp.cumsum(lengths), jnp.arange(rows * top), side="right").astype(jnp.int32)
    table = items.reshape(top, rows).T
    table = table[jax.random.permutation(jax.random.fold_in(own, 1), rows)]
    turn = jax.random.randint(jax.random.fold_in(own, 2), (rows, 1), 0, top)
    return jnp.take_along_axis(table, (jnp.arange(top)[None, :] + turn) % top, axis=1)


def load_shares(number_of, total, bound, slope, full):
    loads = [(1 << 20) // math.isqrt(grade ** slope) + 1 for grade in range(1, number_of + 1)]
    largest = bound if full else min(bound, max(-(-total // number_of), total * loads[0] // sum(loads)))
    least = 1 if total - largest >= number_of - 1 else 0
    counts, surplus = [largest] + [least] * (number_of - 1), total - largest - least * (number_of - 1)
    while surplus > 0:
        candidates = [i for i in range(1, number_of) if counts[i] < largest] or [i for i in range(1, number_of) if counts[i] < bound]
        whole, budget = sum([loads[i] for i in candidates]), surplus
        for i in candidates:
            more = min(bound - counts[i], max(1, budget * loads[i] // whole), surplus)
            counts[i] = counts[i] + more
            surplus = surplus - more
    return np.array(counts)


def scatter_about(rng, shape, spread, most, cuts=(), held_as=jnp.bfloat16):
    values = jax.random.normal(rng, shape, jnp.float32) * spread
    if len(cuts) > 0:
        values = block_scale(rng, shape, cuts, -0.22, 0.18) * values
    return jnp.clip(values, min=-most, max=most).astype(held_as)


def setup_inputs(seed: int = 0) -> dict:
    keys = jax.random.split(jax.random.key(seed), 10)
    hidden = scatter_about(keys[0], (TOKENS, H), 0.5, 4.0, ((0, 32),))
    output_weight = scatter_about(keys[1], (H, WORDS), H ** -0.5, 0.09375, ((1, 8),))
    owners_keys = jax.random.split(jax.random.fold_in(keys[2], 1), TOKENS // TOK_DEV)
    owners_turns = jax.random.permutation(jax.random.fold_in(keys[2], 3), TOKENS // TOK_DEV)
    owners = jax.vmap(lambda own, number: assign_block(jax.random.fold_in(keys[2], 2), own, number, TOK_DEV, N_VOCAB, VIS, CAP, 2))(owners_keys, owners_turns).reshape((TOKENS, VIS))
    negatives = set_ends(jax.random.randint(keys[3], (TOKENS, VIS, PER_OWN), 0, BLK_DEV), jax.random.fold_in(keys[3], 1), 0, BLK_DEV - 1).astype(jnp.int32)
    negative_mask = set_ends((jax.random.randint(keys[4], (TOKENS, VIS, PER_OWN), 0, 4) < 3).astype(jnp.int32), jax.random.fold_in(keys[4], 1), 0, 1)
    target_block = set_ends(jax.random.randint(keys[5], (TOKENS,), 0, BLK_DEV), jax.random.fold_in(keys[5], 1), 0, BLK_DEV - 1).astype(jnp.int32)
    target_word = set_ends(jax.random.randint(keys[6], (TOKENS,), 0, BLOCK), jax.random.fold_in(keys[6], 1), 0, BLOCK - 1).astype(jnp.int32)
    log_norm = jnp.clip(1.0 + 1.0 * jax.random.uniform(keys[7], (TOKENS,), jnp.float32) ** block_scale(keys[7], (TOKENS,), ((0, 32),), -0.2, 0.2), 1.0, 2.0).astype(jnp.bfloat16)
    cotangent = jnp.clip(4.0 + 4.0 * jax.random.uniform(keys[8], (TOKENS,), jnp.float32) ** block_scale(keys[8], (TOKENS,), ((0, 32),), -0.2, 0.2), 4.0, 8.0).astype(jnp.bfloat16)
    return dict(hidden=hidden, output_weight=output_weight, owners=owners, negatives=negatives, negative_mask=negative_mask, target_block=target_block, target_word=target_word, log_norm=log_norm, cotangent=cotangent)


def reference(hidden, output_weight, owners, negatives, negative_mask, target_block, target_word, log_norm, cotangent):
    owner_words = BLK_DEV * BLOCK
    entries = GROUP_TOK * VIS
    reach = N_VOCAB * CAP
    word_position = jnp.arange(owner_words).astype(jnp.float32)
    cluster_ids = jnp.arange(BLK_DEV).astype(jnp.int32)

    def group_step(weight_acc, group):
        first_row = group * GROUP_TOK

        def take_group(array):
            return lax.dynamic_slice_in_dim(array, first_row, GROUP_TOK, 0)

        group_hidden = take_group(hidden)
        flat_owner = take_group(owners).reshape(entries)
        group_negative = take_group(negatives).reshape(entries, PER_OWN)
        group_mask = take_group(negative_mask).reshape(entries, PER_OWN)
        group_block = take_group(target_block)
        group_word = take_group(target_word)
        group_norm = take_group(log_norm)
        group_cotangent = take_group(cotangent)

        def owner_step(owner):
            chosen = jnp.nonzero(flat_owner == owner, size=reach, fill_value=entries)[0].astype(jnp.int32)
            valid = chosen < entries
            safe_index = jnp.minimum(chosen, entries - 1)
            token_of = safe_index // VIS
            is_first = (safe_index % VIS) == 0
            token_rows = jnp.where(valid[:, None], group_hidden[token_of], 0).astype(jnp.bfloat16)
            columns = lax.dynamic_slice_in_dim(output_weight, owner * owner_words, owner_words, 1)
            scores = jnp.dot(token_rows, columns, preferred_element_type=jnp.float32)
            picked_negative = group_negative[safe_index]
            picked_mask = group_mask[safe_index]
            target_here = jnp.where(is_first, group_block[token_of], -1)
            matched = (picked_negative[:, :, None] == cluster_ids[None, None, :]) & (picked_mask[:, :, None] == 1)
            cluster_counts = jnp.sum(jnp.where(matched, 1.0, 0.0), axis=1) + jnp.where(target_here[:, None] == cluster_ids[None, :], 1.0, 0.0)
            word_counts = jnp.repeat(cluster_counts, BLOCK, axis=1)
            target_col = (target_here * BLOCK + group_word[token_of]).astype(jnp.float32)
            token_weight = jnp.where(valid, group_cotangent[token_of].astype(jnp.float32), 0.0)
            log_total = group_norm[token_of].astype(jnp.float32)
            target_hot = jnp.where(word_position[None, :] == target_col[:, None], 1.0, 0.0)
            score_grad = (token_weight[:, None] * (word_counts * jnp.exp(scores - log_total[:, None]) - target_hot)).astype(jnp.bfloat16)
            grad_rows = jnp.dot(score_grad, columns.T, preferred_element_type=jnp.float32).astype(jnp.bfloat16)
            weight_part = jnp.dot(token_rows.T, score_grad, preferred_element_type=jnp.float32).astype(jnp.bfloat16)
            return grad_rows, chosen, weight_part

        grad_rows, chosen, weight_part = lax.map(owner_step, jnp.arange(N_VOCAB).astype(jnp.int32))
        per_entry = jnp.zeros((entries, H), jnp.float32).at[chosen.reshape(-1)].set(grad_rows.reshape(-1, H).astype(jnp.float32), mode="drop")
        hidden_group = jnp.sum(per_entry.reshape(GROUP_TOK, VIS, H), axis=1).astype(jnp.bfloat16)
        weight_acc = weight_acc + jnp.moveaxis(weight_part, 0, 1).reshape(H, N_VOCAB * owner_words).astype(jnp.float32)
        return weight_acc, hidden_group

    weight_acc, hidden_parts = lax.scan(group_step, jnp.zeros((H, WORDS), jnp.float32), jnp.arange(N_DP).astype(jnp.int32))
    return hidden_parts.reshape(TOKENS, H), weight_acc.astype(jnp.bfloat16)
```

```python
import jax
import jax.numpy as jnp
from jax import lax
from jax.experimental import pallas as pl
from jax.experimental.pallas import tpu as pltpu
from jax.sharding import PartitionSpec as P

BLOCK = 128
BLK_DEV = 8
F32 = jnp.float32
BF16 = jnp.bfloat16


MESH = pl.DeviceIdType.MESH
CUBE = 8
LINE = 4
TILE = 8
NT = (((1,), (1,)), ((), ()))


def rows_at(start, count):
    return pl.ds(pl.multiple_of(start, count), count)


def make_facts(own_ref, neg_ref, mask_ref, block_ref, word_ref, norm_ref, cot_ref):
    visits, tokens = own_ref.shape
    per_own = neg_ref.shape[1]
    kinds = per_own + 1
    row = lax.broadcasted_iota(jnp.int32, (TILE, tokens), 0)
    owners = own_ref[...].astype(F32)
    code = jnp.where(mask_ref[...] == 1, neg_ref[...] + 1, 0).astype(F32)
    extra = [
        word_ref[...].astype(F32),
        norm_ref[...].astype(F32),
        cot_ref[...].astype(F32),
        jnp.ones((1, tokens), F32),
    ]
    owner_tiles, code_tiles = [], []
    for v in range(visits):
        owner_tiles.append(jnp.broadcast_to(owners[v : v + 1, :], (TILE, tokens)))
        lines = [block_ref[...].astype(F32) + 1.0 if v == 0 else jnp.zeros((1, tokens), F32)]
        lines += [code[v, n : n + 1, :] for n in range(per_own)] + extra
        tile = jnp.zeros((TILE, tokens), F32)
        for i, line in enumerate(lines):
            tile = jnp.where(row == i, jnp.broadcast_to(line, (TILE, tokens)), tile)
        code_tiles.append(tile)
    return jnp.concatenate(owner_tiles + code_tiles, axis=0).astype(BF16)


def read_facts(facts, me, kinds, visits):
    f = facts.astype(F32)
    sources, _, tokens = f.shape
    rows = visits * TILE
    mine = jnp.where(f[:, :rows, :] == me.astype(F32), f[:, rows:, :], 0.0)
    cand = mine[:, :TILE, :]
    for v in range(1, visits):
        cand = cand + mine[:, v * TILE : (v + 1) * TILE, :]
    row = lax.broadcasted_iota(jnp.int32, cand.shape, 1)
    only = cand
    for k in range(kinds - 1):
        earlier = jnp.broadcast_to(cand[:, k : k + 1, :], cand.shape)
        only = jnp.where((row > k) & (row < kinds) & (cand == earlier), 0.0, only)
    before = lax.broadcasted_iota(jnp.int32, (tokens, tokens), 0)
    after = lax.broadcasted_iota(jnp.int32, (tokens, tokens), 1)
    upper = jnp.where(before < after, 1.0, 0.0).astype(BF16)
    flat = cand.reshape(sources * TILE, tokens).astype(BF16)
    rank = jnp.dot(flat, upper, preferred_element_type=F32).reshape(cand.shape)
    place = jnp.where(cand > 0.0, rank, -1.0)
    return cand, only, place


def pick_of(place_ref, m, s, line, capacity):
    tokens = place_ref.shape[3]
    place = place_ref[m, s][line : line + 1, :]
    slot = lax.broadcasted_iota(jnp.int32, (capacity, tokens), 0).astype(F32)
    return jnp.where(jnp.broadcast_to(place, (capacity, tokens)) == slot, 1.0, 0.0).astype(BF16)


def chip_scores(c, kinds, g, w, cols, grads, pk):
    count = pk.shape[0]
    words = w.shape[1]
    pair = 2 * BLOCK
    at = rows_at(c * count, count)
    lane = lax.broadcasted_iota(jnp.int32, (count, BLOCK), 1).astype(F32)
    pk[...] = jnp.zeros_like(pk)

    @pl.loop(0, words // pair)
    def _(j):
        words_at = rows_at(j * pair, pair)
        scores = jnp.dot(g[at, :], w[:, words_at], preferred_element_type=F32)
        col = [jnp.broadcast_to(cols[at, i : i + 1], (count, BLOCK)) for i in range(kinds + 3)]
        only = [
            jnp.broadcast_to(cols[at, TILE + i : TILE + i + 1], (count, BLOCK))
            for i in range(kinds)
        ]
        word, norm, cot = col[kinds:]
        here = jnp.where(word == lane, 1.0, 0.0)
        sides = []
        for i in range(2):
            block = (2 * j + i + 1).astype(F32)
            counts = jnp.where(col[0] == block, 1.0, 0.0)
            hot = counts * here
            for k in range(1, kinds):
                counts = counts + jnp.where(col[k] == block, 1.0, 0.0)
            score = scores[:, i * BLOCK : (i + 1) * BLOCK]
            grown = jnp.where(counts > 0.0, counts * jnp.exp(score - norm), 0.0)
            grad = cot * (grown - hot)
            for k in range(kinds):
                spot = slice(k * BLOCK, (k + 1) * BLOCK)
                pk[:, spot] = jnp.where(only[k] == block, grad, pk[:, spot])
            sides.append(grad.astype(BF16))
        grads[at, words_at] = jnp.concatenate(sides, axis=1)


def chip_back(c, count, w, grads, b):
    width = w.shape[0]
    step = min(512, width)
    at = rows_at(c * count, count)

    @pl.loop(0, width // step)
    def _(j):
        cut = rows_at(j * step, step)
        b[at, cut] = lax.dot_general(
            grads[at, :], w[cut, :], NT, preferred_element_type=F32
        ).astype(BF16)


def add_product(lhs_t, spread, acc, out=None, first=False):
    pair = 2 * BLOCK

    @pl.loop(0, acc.shape[1] // pair)
    def _(j):
        at = rows_at(j * pair, pair)
        value = jnp.dot(lhs_t[...], spread(j, at), preferred_element_type=F32)
        if not first:
            value = value + acc[:, at]
        if out is None:
            acc[:, at] = value
        else:
            out[:, at] = value.astype(BF16)


def unpack(kinds, only_cols, packed):
    def spread(j, _):
        sides = []
        for i in range(2):
            block = (2 * j + i + 1).astype(F32)
            value = None
            for k in range(kinds):
                mine = jnp.broadcast_to(only_cols[:, k : k + 1], (only_cols.shape[0], BLOCK)) == block
                term = packed(k).astype(F32)
                value = jnp.where(mine, term, 0.0 if value is None else value)
            sides.append(value.astype(BF16))
        return jnp.concatenate(sides, axis=1)

    return spread


def flip(value, m):
    bit, out = 1, value
    while bit <= m:
        if m & bit:
            out = out + bit - 2 * bit * ((value // bit) % 2)
        bit *= 2
    return out


def cube_kernel(
    n_dp,
    h_ref,
    w_ref,
    own_ref,
    neg_ref,
    mask_ref,
    block_ref,
    word_ref,
    norm_ref,
    cot_ref,
    o_ref,
    wg_ref,
    w,
    g,
    b,
    sbuf,
    sums,
    hx,
    hy,
    fx,
    fy,
    facts,
    place,
    only,
    cols,
    only_cols,
    grads,
    pk,
    packed,
    parts,
    near_out,
    near_in,
    lhs,
    lhs_t,
    acc,
    send,
    recv,
    local,
):
    v = lax.axis_index("vocab")
    dp = lax.axis_index("dp")
    sib, xp, yp = flip(v, 1), flip(v, 2), flip(v, 4)
    diag = flip(v, 6)
    chip, xc, yc, dc = v // 2, xp // 2, yp // 2, diag // 2
    tokens, width = h_ref.shape
    visits, per_own = neg_ref.shape[:2]
    kinds = per_own + 1
    part = width // n_dp
    half = tokens // 2
    capacity = packed.shape[2]
    count = 2 * tokens
    others = [flip(v, u) for u in range(1, CUBE)]
    groups = [flip(dp, m) for m in range(n_dp)]
    far = range(2, n_dp)
    copies = []

    def push(src, dst, **where):
        i = len(copies)
        copy = pltpu.make_async_remote_copy(
            src_ref=src,
            dst_ref=dst,
            send_sem=send.at[i],
            recv_sem=recv.at[i],
            device_id=where,
            device_id_type=MESH,
        )
        copy.start()
        copies.append(copy)
        return copy

    def wait(*items):
        for copy in items:
            copy.wait_recv()

    def dev_rows(q, first=0, rows=None):
        rows = tokens if rows is None else rows
        return rows_at(q * tokens + first, rows)

    load_w = pltpu.make_async_copy(w_ref, w, local.at[0])
    load_w.start()
    load_h = pltpu.make_async_copy(h_ref, g.at[dev_rows(v)], local.at[1])
    load_h.start()
    facts[0, v] = make_facts(own_ref, neg_ref, mask_ref, block_ref, word_ref, norm_ref, cot_ref)

    barrier = pltpu.get_barrier_semaphore()
    for peer in others:
        pl.semaphore_signal(barrier, inc=1, device_id={"vocab": peer}, device_id_type=MESH)
    for peer in groups[1:]:
        pl.semaphore_signal(barrier, inc=1, device_id={"dp": peer}, device_id_type=MESH)
    pl.semaphore_wait(barrier, CUBE - 1 + n_dp - 1)

    facts_z = [push(facts.at[0, v], facts.at[m, v], dp=groups[m]) for m in range(1, n_dp)]
    facts_in = [push(facts.at[0, v], facts.at[0, v], vocab=peer) for peer in others]
    low, high = pl.ds(0, half), pl.ds(half, half)
    x_low = push(h_ref.at[low], g.at[dev_rows(v, 0, half)], vocab=xp)
    y_high = push(h_ref.at[high], g.at[dev_rows(v, half, half)], vocab=yp)
    x_high = push(h_ref.at[high], g.at[dev_rows(v, half, half)], vocab=xp)
    y_low = push(h_ref.at[low], g.at[dev_rows(v, 0, half)], vocab=yp)
    s_own = push(h_ref, g.at[dev_rows(v)], vocab=sib)
    far_in = []
    for m in far:
        columns = rows_at(groups[m] * part, part)
        far_in.append(push(h_ref.at[:, columns], parts.at[m - 2, v], dp=groups[m]))

    def forward(q, first, rows, **where):
        at = dev_rows(q, first, rows)
        return push(g.at[at], g.at[at], **where)

    wait(*facts_in)
    cand, own_only, own_place = read_facts(facts[0], v, kinds, visits)
    place[0] = own_place
    diagonal = lax.broadcasted_iota(jnp.int32, (tokens, tokens), 0) == lax.broadcasted_iota(
        jnp.int32, (tokens, tokens), 1
    )
    eye = jnp.where(diagonal, 1.0, 0.0).astype(BF16)
    for s in range(CUBE):
        both = jnp.concatenate([cand[s], own_only[s]], axis=0).astype(BF16)
        cols[s * tokens : (s + 1) * tokens, :] = lax.dot_general(
            eye, both, NT, preferred_element_type=F32
        )
    wait(*facts_z)
    facts_out = [push(facts.at[1:, v], facts.at[1:, v], vocab=peer) for peer in others]

    packs_in, near_copies = [], []

    def work(c, service=None):
        chip_scores(c, kinds, g, w, cols, grads, pk)
        near_columns = rows_at(groups[1] * part, part)
        for i in range(2):
            s = 2 * c + i
            pick = pick_of(place, 0, s, kinds + 3, capacity)
            mine = pk[i * tokens : (i + 1) * tokens, :].astype(BF16)
            packed[0, s] = jnp.dot(pick, mine, preferred_element_type=F32).astype(BF16)
            near_out[rows_at(s * capacity, capacity), :] = jnp.dot(
                pick, g[dev_rows(s), near_columns], preferred_element_type=F32
            ).astype(BF16)
        two = pl.ds(2 * c, 2)
        for m in range(1, n_dp):
            packs_in.append(push(packed.at[0, two], packed.at[m, two], dp=groups[m]))
        at = rows_at(2 * c * capacity, 2 * capacity)
        near_copies.append(push(near_out.at[at], near_in.at[at], dp=groups[1]))
        if service is not None:
            service()
        chip_back(c, count, w, grads, b)

    def pair(i, q):
        return push(b.at[dev_rows(flip(q, 1))], sbuf.at[i], vocab=sib)

    load_w.wait()
    load_h.wait()
    wait(s_own)
    work(chip)
    pair_own = pair(3, v)

    wait(x_low)
    d_low = forward(xp, 0, half, vocab=yp)
    s1 = forward(xp, 0, half, vocab=sib)
    wait(y_high)
    d_high = forward(yp, half, half, vocab=xp)
    s2 = forward(yp, half, half, vocab=sib)
    wait(x_high)
    s3 = forward(xp, half, half, vocab=sib)
    wait(y_low)
    s4 = forward(yp, 0, half, vocab=sib)
    wait(s1, s3)

    far_half = max(1, len(far) // 2)
    far_low, far_high = pl.ds(0, far_half), pl.ds(far_half, len(far) - far_half)
    far_copies = []

    def far_direct():
        wait(*far_in)
        for where in (dict(vocab=xp), dict(vocab=yp), dict(vocab=sib)):
            far_copies.append(push(parts.at[:, v], parts.at[:, v], **where))

    work(xc)
    pair_x = pair(1, xp)
    far_direct()
    wait(d_low)
    s5 = forward(diag, 0, half, vocab=sib)
    wait(d_high)
    s6 = forward(diag, half, half, vocab=sib)
    wait(s2, s4)

    def add_sum(i, q, first, hop=None):
        step = 16

        @pl.loop(0, half // step)
        def _(k):
            at = rows_at(first + k * step, step)
            total = b[rows_at(q * tokens + first + k * step, step), :].astype(F32)
            total = total + sbuf[i, at, :].astype(F32)
            if hop is not None:
                total = total + hop[rows_at(k * step, step), :].astype(F32)
            sums[i, at, :] = total.astype(BF16)

    back_copies = []

    def x_back():
        wait(pair_x)
        add_sum(1, xp, 0)
        back_copies.append(push(sums.at[1, low], fx.at[low], vocab=xp))

    work(yc, x_back)
    pair_y = pair(2, yp)
    wait(s5, s6)

    def y_back():
        wait(pair_y)
        add_sum(2, yp, half)
        back_copies.append(push(sums.at[2, high], fy.at[high], vocab=yp))

    work(dc, y_back)
    pair_d = pair(0, diag)
    wait(pair_d)
    add_sum(0, diag, 0)
    to_x = push(sums.at[0, low], hx, vocab=xp)
    add_sum(0, diag, half)
    to_y = push(sums.at[0, high], hy, vocab=yp)

    wait(*far_copies)
    far_on = [
        push(parts.at[far_low, xp], parts.at[far_low, xp], vocab=yp),
        push(parts.at[far_high, yp], parts.at[far_high, yp], vocab=xp),
    ]
    far_sib = [push(parts.at[:, q], parts.at[:, q], vocab=sib) for q in (xp, yp)]

    chunk = lhs.shape[0]
    own_columns = rows_at(dp * part, part)
    for i in range(CUBE * tokens // chunk):
        at = slice(i * chunk, (i + 1) * chunk)
        lhs_t[...] = g[at, own_columns].T
        add_product(lhs_t, lambda j, words_at, at=at: grads[at, words_at], acc, first=i == 0)

    wait(to_y)
    add_sum(1, xp, half, hy)
    back_copies.append(push(sums.at[1, high], fx.at[high], vocab=xp))
    wait(to_x)
    add_sum(2, yp, 0, hx)
    back_copies.append(push(sums.at[2, low], fy.at[low], vocab=yp))

    wait(*far_on)
    far_sib += [
        push(parts.at[far_low, diag], parts.at[far_low, diag], vocab=sib),
        push(parts.at[far_high, diag], parts.at[far_high, diag], vocab=sib),
    ]

    wait(*facts_out)
    wait(*packs_in)
    wait(*near_copies)
    wait(*far_sib)
    for m in range(1, n_dp):
        _, other_only, other_place = read_facts(facts[m], v, kinds, visits)
        place[m] = other_place
        only[...] = other_only

        @pl.loop(0, CUBE)
        def _(s):
            at = rows_at(s * capacity, capacity)
            pick = pick_of(place, m, s, kinds + 3, capacity)
            only_cols[at, :] = lax.dot_general(
                pick, only[s].astype(BF16), NT, preferred_element_type=F32
            )
            if m > 1:
                lhs[at, :] = jnp.dot(
                    pick, parts[m - 2, s], preferred_element_type=F32
                ).astype(BF16)

        lhs_t[...] = (near_in if m == 1 else lhs)[...].T

        def block_of(k, m=m):
            return packed[m, :, :, k * BLOCK : (k + 1) * BLOCK].reshape(CUBE * capacity, BLOCK)

        add_product(
            lhs_t, unpack(kinds, only_cols, block_of), acc, out=wg_ref if m == n_dp - 1 else None
        )

    wait(pair_own, *back_copies)
    step = 16

    @pl.loop(0, tokens // step)
    def _(k):
        at = rows_at(k * step, step)
        total = b[rows_at(v * tokens + k * step, step), :].astype(F32)
        total = total + sbuf[3, at, :].astype(F32)
        total = total + fx[at, :].astype(F32) + fy[at, :].astype(F32)
        o_ref[at, :] = total.astype(BF16)

    for copy in copies:
        copy.wait_send()


def cube_program(
    hidden, weight, owners, negatives, mask, block, word, norm, cot, n_dp, capacity
):
    tokens, width = hidden.shape
    words = weight.shape[1]
    visits, per_own = negatives.shape[1:]
    part = width // n_dp
    slots = CUBE * capacity
    group = CUBE * tokens
    kinds = per_own + 1
    vmem = pl.BlockSpec(memory_space=pltpu.VMEM)
    hbm = pl.BlockSpec(memory_space=pl.ANY)
    v = pltpu.VMEM
    total = 96
    return pl.pallas_call(
        lambda *refs: cube_kernel(n_dp, *refs),
        out_shape=(
            jax.ShapeDtypeStruct((tokens, width), BF16),
            jax.ShapeDtypeStruct((part, words), BF16),
        ),
        in_specs=[hbm, hbm] + [vmem] * 7,
        out_specs=(vmem, vmem),
        scratch_shapes=[
            v((width, words), BF16),
            v((group, width), BF16),
            v((group, width), BF16),
            v((4, tokens, width), BF16),
            v((3, tokens, width), BF16),
            v((tokens // 2, width), BF16),
            v((tokens // 2, width), BF16),
            v((tokens, width), BF16),
            v((tokens, width), BF16),
            v((n_dp, CUBE, 2 * visits * TILE, tokens), BF16),
            v((n_dp, CUBE, TILE, tokens), F32),
            v((CUBE, TILE, tokens), F32),
            v((group, 2 * TILE), F32),
            v((slots, TILE), F32),
            v((group, words), BF16),
            v((2 * tokens, kinds * BLOCK), F32),
            v((n_dp, CUBE, capacity, kinds * BLOCK), BF16),
            v((n_dp - 2, CUBE, tokens, part), BF16),
            v((slots, part), BF16),
            v((slots, part), BF16),
            v((slots, part), BF16),
            v((part, slots), BF16),
            v((part, words), F32),
            pltpu.SemaphoreType.DMA((total,)),
            pltpu.SemaphoreType.DMA((total,)),
            pltpu.SemaphoreType.DMA((2,)),
        ],
        compiler_params=pltpu.CompilerParams(
            collective_id=0, has_side_effects=True, vmem_limit_bytes=62 * 2**20
        ),
        name="cube",
    )(
        hidden,
        weight,
        owners.T,
        jnp.transpose(negatives, (1, 2, 0)),
        jnp.transpose(mask, (1, 2, 0)),
        block[None, :],
        word[None, :],
        norm[None, :],
        cot[None, :],
    )


def weight_kernel(own_ref, pick_ref, part_ref, packed_ref, only_ref, o_ref, lhs, lhs_t, acc):
    g = pl.program_id(0)
    sources, capacity = pick_ref.shape[:2]
    kinds = only_ref.shape[1]
    pair = 2 * BLOCK

    @pl.when(g == 0)
    def _():
        lhs[...] = own_ref[...]
        acc[...] = jnp.zeros_like(acc)

    @pl.when(g > 0)
    def _():
        for s in range(sources):
            lhs[s * capacity : (s + 1) * capacity, :] = jnp.dot(
                pick_ref[s], part_ref[0, s], preferred_element_type=F32
            ).astype(BF16)

    lhs_t[...] = lhs[...].T

    @pl.loop(0, acc.shape[1] // pair, unroll=True)
    def _(j):
        sides = []
        for i in range(2):
            block = (2 * j + i + 1).astype(F32)
            value = jnp.zeros((lhs.shape[0], BLOCK), F32)
            for k in range(kinds):
                value = jnp.where(
                    only_ref[:, k : k + 1] == block,
                    packed_ref[0, :, k * BLOCK : (k + 1) * BLOCK].astype(F32),
                    value,
                )
            sides.append(value.astype(BF16))
        spread = jnp.concatenate(sides, axis=1)
        at = pl.ds(pl.multiple_of(j * pair, pair), pair)
        acc[:, at] += jnp.dot(lhs_t[...], spread, preferred_element_type=F32)

    @pl.when(g == pl.num_programs(0) - 1)
    def _():
        o_ref[...] = acc[...].astype(BF16)


def weight_product(own, pick, parts, packed, only, words):
    groups, slots = packed.shape[:2]
    _, sources, tokens, part = parts.shape
    capacity = pick.shape[1]
    kinds = only.shape[1]
    return pl.pallas_call(
        weight_kernel,
        grid=(groups,),
        out_shape=jax.ShapeDtypeStruct((part, words), BF16),
        in_specs=[
            pl.BlockSpec((slots, part), lambda g: (0, 0)),
            pl.BlockSpec((sources, capacity, tokens), lambda g: (jnp.maximum(g - 1, 0), 0, 0)),
            pl.BlockSpec((1, sources, tokens, part), lambda g: (jnp.maximum(g - 1, 0), 0, 0, 0)),
            pl.BlockSpec((1, slots, packed.shape[2]), lambda g: (g, 0, 0)),
            pl.BlockSpec((slots, kinds), lambda g: (g, 0)),
        ],
        out_specs=pl.BlockSpec((part, words), lambda g: (0, 0)),
        scratch_shapes=[
            pltpu.VMEM((slots, part), BF16),
            pltpu.VMEM((part, slots), BF16),
            pltpu.VMEM((part, words), F32),
        ],
        compiler_params=pltpu.CompilerParams(dimension_semantics=("arbitrary",)),
        name="weight_product",
    )(own, pick, parts, packed, only)


def body(
    hidden,
    output_weight,
    owners,
    negatives,
    negative_mask,
    target_block,
    target_word,
    log_norm,
    cotangent,
):
    tokens, width = hidden.shape
    visits = owners.shape[1]
    per_own = negatives.shape[2]
    n_vocab = lax.axis_size("vocab")
    n_dp = lax.axis_size("dp")
    me = lax.axis_index("vocab")
    my_dp = lax.axis_index("dp")
    words = output_weight.shape[1]
    capacity = max(2, tokens * visits * 4 // (3 * n_vocab))
    if n_vocab == CUBE and n_dp == LINE:
        return cube_program(
            hidden,
            output_weight,
            owners,
            negatives,
            negative_mask,
            target_block,
            target_word,
            log_norm,
            cotangent,
            n_dp,
            capacity,
        )
    slots = n_vocab * capacity
    part = width // n_dp

    facts = jnp.concatenate(
        [
            owners.T,
            negatives.reshape(tokens, -1).T,
            negative_mask.reshape(tokens, -1).T,
            target_block[None, :],
            target_word[None, :],
        ],
        axis=0,
    ).astype(BF16)
    facts = jnp.concatenate([facts, log_norm[None, :], cotangent[None, :]], axis=0)
    facts = jnp.pad(facts, ((0, -facts.shape[0] % 16), (0, 0)))
    blocks = n_dp * n_vocab

    group_rows = lax.all_gather(hidden, "vocab", axis=0, tiled=False)
    part_rows = lax.all_to_all(hidden, "dp", split_axis=1, concat_axis=0, tiled=True)
    part_rows = jnp.roll(part_rows.reshape(n_dp, tokens, part), -my_dp, axis=0)[1:]
    facts = lax.all_gather(lax.all_gather(facts, "dp", axis=0), "vocab", axis=0)
    facts = jnp.roll(facts, -my_dp, axis=1)
    part_rows = lax.all_gather(part_rows, "vocab", axis=1)
    facts = jnp.swapaxes(facts, 0, 1).reshape(blocks, -1, tokens)

    f = facts.astype(F32)
    pairs = visits * per_own
    hit = f[:, :visits, :] == me.astype(F32)
    neg = f[:, visits : visits + pairs, :]
    mask = f[:, visits + pairs : visits + 2 * pairs, :]
    base = visits + 2 * pairs
    t_block, t_word, norm, cot = (f[:, base + i, :] for i in range(4))
    named = jnp.any(hit, axis=1)
    cand = [jnp.where(hit[:, 0], t_block + 1.0, 0.0)]
    for n in range(per_own):
        value = jnp.zeros_like(t_block)
        for v in range(visits):
            i = v * per_own + n
            value = jnp.where(hit[:, v] & (mask[:, i] == 1.0), neg[:, i] + 1.0, value)
        cand.append(value)
    only = []
    for k, value in enumerate(cand):
        for earlier in cand[:k]:
            value = jnp.where(value == earlier, 0.0, value)
        only.append(value)
    upper = jnp.triu(jnp.ones((tokens, tokens), BF16), 1)
    rank = jnp.dot(named.astype(BF16), upper, preferred_element_type=F32)
    place = jnp.where(named, rank, -1.0)
    pick = (
        place[:, None, :] == jnp.arange(capacity, dtype=jnp.int32).astype(F32)[None, :, None]
    ).astype(BF16)
    attrs = jnp.stack(cand + only + [t_word, norm, cot], axis=1).astype(BF16)
    slot_facts = jnp.einsum("sct,sat->sca", pick, attrs, preferred_element_type=F32)
    kinds = per_own + 1
    all_only = slot_facts[:, :, kinds : 2 * kinds].reshape(n_dp * slots, kinds)
    mine = slot_facts[:n_vocab].reshape(slots, -1)
    my_pick = pick[:n_vocab]

    rows = jnp.einsum("sct,sth->sch", my_pick, group_rows, preferred_element_type=F32)
    rows = rows.astype(BF16).reshape(slots, width)
    scores = jnp.dot(rows, output_weight, preferred_element_type=F32)
    word_ids = jnp.arange(words, dtype=jnp.int32)[None, :]
    word_block = (word_ids // BLOCK + 1).astype(F32)
    word_in = (word_ids % BLOCK).astype(F32)
    counts = jnp.zeros((slots, words), F32)
    for k in range(kinds):
        counts = counts + jnp.where(mine[:, k : k + 1] == word_block, 1.0, 0.0)
    hot = jnp.where(
        (mine[:, 0:1] == word_block) & (mine[:, 2 * kinds : 2 * kinds + 1] == word_in), 1.0, 0.0
    )
    norm_col = mine[:, 2 * kinds + 1 : 2 * kinds + 2]
    cot_col = mine[:, 2 * kinds + 2 : 2 * kinds + 3]
    grown = jnp.where(counts > 0.0, counts * jnp.exp(scores - norm_col), 0.0)
    grad = (cot_col * (grown - hot)).astype(BF16)

    packed = []
    for k in range(kinds):
        which = mine[:, kinds + k : kinds + k + 1]
        value = jnp.zeros((slots, BLOCK), BF16)
        for b in range(BLK_DEV):
            value = jnp.where(which == b + 1.0, grad[:, b * BLOCK : (b + 1) * BLOCK], value)
        packed.append(value)
    packed = jnp.concatenate(packed, axis=1)
    back = lax.dot_general(
        grad, output_weight, (((1,), (1,)), ((), ())), preferred_element_type=F32
    ).astype(BF16)
    back = jnp.einsum(
        "sct,sch->sth", my_pick, back.reshape(n_vocab, capacity, width), preferred_element_type=F32
    ).astype(BF16)
    hidden_grad = lax.psum_scatter(
        back.reshape(n_vocab * tokens, width), "vocab", scatter_dimension=0, tiled=True
    )
    packed = jnp.roll(lax.all_gather(packed, "dp", axis=0), -my_dp, axis=0)
    own_slots = lax.dynamic_slice_in_dim(rows, my_dp * part, part, 1)
    weight_grad = weight_product(own_slots, pick[n_vocab:], part_rows, packed, all_only, words)
    return (hidden_grad, weight_grad)


def solution(mesh):
    placed = (
        P(("dp", "vocab"), None),
        P(None, "vocab"),
        P(("dp", "vocab"), None),
        P(("dp", "vocab"), None, None),
        P(("dp", "vocab"), None, None),
        P(("dp", "vocab")),
        P(("dp", "vocab")),
        P(("dp", "vocab")),
        P(("dp", "vocab")),
    )
    return jax.shard_map(
        body,
        mesh=mesh,
        in_specs=placed,
        out_specs=(P(("dp", "vocab"), None), P("dp", "vocab")),
        check_vma=False,
    )
```

```python
import jax
import jax.numpy as jnp
from jax import lax
from jax.experimental import pallas as pl
from jax.experimental.pallas import tpu as pltpu
from jax.sharding import PartitionSpec as P

BLOCK = 128
BLK_DEV = 8
F32 = jnp.float32
BF16 = jnp.bfloat16


MESH = pl.DeviceIdType.MESH
CUBE = 8
LINE = 4
TILE = 8
NT = (((1,), (1,)), ((), ()))


def rows_at(start, count):
    return pl.ds(pl.multiple_of(start, count), count)


def make_facts(own_ref, neg_ref, mask_ref, block_ref, word_ref, norm_ref, cot_ref):
    visits, tokens = own_ref.shape
    per_own = neg_ref.shape[1]
    code = jnp.where(mask_ref[...] == 1, neg_ref[...] + 1, 0).astype(F32)
    owners = own_ref[...].astype(F32)
    lines = [owners[v : v + 1, :] for v in range(visits)] + [block_ref[...].astype(F32) + 1.0]
    lines += [code[v, n : n + 1, :] for v in range(visits) for n in range(per_own)]
    lines += [ref[...].astype(F32) for ref in (word_ref, norm_ref, cot_ref)]
    count = fact_rows(visits, per_own)
    row = lax.broadcasted_iota(jnp.int32, (count, tokens), 0)
    tile = jnp.zeros((count, tokens), F32)
    for i, line in enumerate(lines):
        tile = jnp.where(row == i, jnp.broadcast_to(line, (count, tokens)), tile)
    return tile.astype(BF16)


def fact_rows(visits, per_own):
    rows = visits * (1 + per_own) + 4
    return rows + -rows % (2 * TILE)


def read_facts(facts, me, visits, per_own):
    f = facts.astype(F32)
    sources, _, tokens = f.shape
    kinds = per_own + 1
    line = lambda i: f[:, i : i + 1, :]
    hit = [jnp.where(line(v) == me.astype(F32), 1.0, 0.0) for v in range(visits)]
    named = sum(hit[1:], hit[0])
    lines = [hit[0] * line(visits)]
    for n in range(per_own):
        terms = [hit[v] * line(visits + 1 + v * per_own + n) for v in range(visits)]
        lines.append(sum(terms[1:], terms[0]))
    base = visits + 1 + visits * per_own
    lines += [named * line(base + i) for i in range(3)] + [named]
    row = lax.broadcasted_iota(jnp.int32, (sources, TILE, tokens), 1)
    cand = jnp.zeros((sources, TILE, tokens), F32)
    for i, value in enumerate(lines):
        cand = jnp.where(row == i, jnp.broadcast_to(value, cand.shape), cand)
    only = cand
    for k in range(kinds - 1):
        earlier = jnp.broadcast_to(lines[k], cand.shape)
        only = jnp.where((row > k) & (row < kinds) & (cand == earlier), 0.0, only)
    before = lax.broadcasted_iota(jnp.int32, (tokens, tokens), 0)
    after = lax.broadcasted_iota(jnp.int32, (tokens, tokens), 1)
    upper = jnp.where(before < after, 1.0, 0.0).astype(BF16)
    flat = cand.reshape(sources * TILE, tokens).astype(BF16)
    rank = jnp.dot(flat, upper, preferred_element_type=F32).reshape(cand.shape)
    place = jnp.where(cand > 0.0, rank, -1.0)
    return cand, only, place


def pick_of(place_ref, s, line, slots):
    tokens = place_ref.shape[2]
    place = place_ref[s][line : line + 1, :]
    slot = lax.broadcasted_iota(jnp.int32, (slots, tokens), 0).astype(F32)
    return jnp.where(jnp.broadcast_to(place, (slots, tokens)) == slot, 1.0, 0.0).astype(BF16)


def chip_scores(c, kinds, g, w, cols, grads, pk):
    count = pk.shape[0]
    words = w.shape[1]
    pair = 2 * BLOCK
    at = rows_at(c * count, count)
    lane = lax.broadcasted_iota(jnp.int32, (count, BLOCK), 1).astype(F32)
    pk[...] = jnp.zeros_like(pk)

    @pl.loop(0, words // pair)
    def _(j):
        words_at = rows_at(j * pair, pair)
        scores = jnp.dot(g[at, :], w[:, words_at], preferred_element_type=F32)
        col = [jnp.broadcast_to(cols[at, i : i + 1], (count, BLOCK)) for i in range(kinds + 3)]
        only = [
            jnp.broadcast_to(cols[at, TILE + i : TILE + i + 1], (count, BLOCK))
            for i in range(kinds)
        ]
        word, norm, cot = col[kinds:]
        here = jnp.where(word == lane, 1.0, 0.0)
        sides = []
        for i in range(2):
            block = (2 * j + i + 1).astype(F32)
            counts = jnp.where(col[0] == block, 1.0, 0.0)
            hot = counts * here
            for k in range(1, kinds):
                counts = counts + jnp.where(col[k] == block, 1.0, 0.0)
            score = scores[:, i * BLOCK : (i + 1) * BLOCK]
            grown = jnp.where(counts > 0.0, counts * jnp.exp(score - norm), 0.0)
            grad = cot * (grown - hot)
            for k in range(kinds):
                spot = slice(k * BLOCK, (k + 1) * BLOCK)
                pk[:, spot] = jnp.where(only[k] == block, grad, pk[:, spot])
            sides.append(grad.astype(BF16))
        grads[at, words_at] = jnp.concatenate(sides, axis=1)


def chip_back(c, count, w, grads, b):
    width = w.shape[0]
    step = min(512, width)
    at = rows_at(c * count, count)

    @pl.loop(0, width // step)
    def _(j):
        cut = rows_at(j * step, step)
        b[at, cut] = lax.dot_general(
            grads[at, :], w[cut, :], NT, preferred_element_type=F32
        ).astype(BF16)


def add_product(lhs_t, spread, acc, out=None, first=False):
    pair = 2 * BLOCK

    @pl.loop(0, acc.shape[1] // pair)
    def _(j):
        at = rows_at(j * pair, pair)
        value = jnp.dot(lhs_t[...], spread(j, at), preferred_element_type=F32)
        if not first:
            value = value + acc[:, at]
        if out is None:
            acc[:, at] = value
        else:
            out[:, at] = value.astype(BF16)


def unpack(kinds, only_cols, packed):
    def spread(j, _):
        sides = []
        for i in range(2):
            block = (2 * j + i + 1).astype(F32)
            value = None
            for k in range(kinds):
                mine = jnp.broadcast_to(only_cols[:, k : k + 1], (only_cols.shape[0], BLOCK)) == block
                term = packed(k).astype(F32)
                value = jnp.where(mine, term, 0.0 if value is None else value)
            sides.append(value.astype(BF16))
        return jnp.concatenate(sides, axis=1)

    return spread


def flip(value, m):
    bit, out = 1, value
    while bit <= m:
        if m & bit:
            out = out + bit - 2 * bit * ((value // bit) % 2)
        bit *= 2
    return out


def cube_kernel(
    n_dp,
    h_ref,
    w_ref,
    own_ref,
    neg_ref,
    mask_ref,
    block_ref,
    word_ref,
    norm_ref,
    cot_ref,
    o_ref,
    wg_ref,
    own_in,
    neg_in,
    mask_in,
    block_in,
    word_in,
    norm_in,
    cot_in,
    w,
    g,
    b,
    sbuf,
    sums,
    hx,
    hy,
    fx,
    fy,
    facts,
    place,
    ship,
    cols,
    only_cols,
    grads,
    pk,
    packed,
    parts,
    near_out,
    near_in,
    lhs,
    lhs_t,
    acc,
    send,
    recv,
    local,
):
    v = lax.axis_index("vocab")
    dp = lax.axis_index("dp")
    sib, xp, yp = flip(v, 1), flip(v, 2), flip(v, 4)
    diag = flip(v, 6)
    chip, xc, yc, dc = v // 2, xp // 2, yp // 2, diag // 2
    tokens, width = h_ref.shape
    visits, per_own = neg_in.shape[:2]
    kinds = per_own + 1
    part = width // n_dp
    half = tokens // 2
    capacity = packed.shape[2]
    count = 2 * tokens
    others = [flip(v, u) for u in range(1, CUBE)]
    groups = [flip(dp, m) for m in range(n_dp)]
    far = range(2, n_dp)
    copies = []

    barrier = pltpu.get_barrier_semaphore()
    for peer in others:
        pl.semaphore_signal(barrier, inc=1, device_id={"vocab": peer}, device_id_type=MESH)
    for peer in groups[1:]:
        pl.semaphore_signal(barrier, inc=1, device_id={"dp": peer}, device_id_type=MESH)

    def push(src, dst, **where):
        i = len(copies)
        copy = pltpu.make_async_remote_copy(
            src_ref=src,
            dst_ref=dst,
            send_sem=send.at[i],
            recv_sem=recv.at[i],
            device_id=where,
            device_id_type=MESH,
        )
        copy.start()
        copies.append(copy)
        return copy

    def wait(*items):
        for copy in items:
            copy.wait_recv()

    def dev_rows(q, first=0, rows=None):
        rows = tokens if rows is None else rows
        return rows_at(q * tokens + first, rows)

    codes_in = (own_in, neg_in, mask_in, block_in, word_in, norm_in, cot_in)
    loads = []
    for i, (src, dst) in enumerate(
        zip(
            (own_ref, neg_ref, mask_ref, block_ref, word_ref, norm_ref, cot_ref),
            codes_in,
        )
    ):
        loads.append(pltpu.make_async_copy(src, dst, local.at[2 + i]))
        loads[-1].start()
    load_h = pltpu.make_async_copy(h_ref, g.at[dev_rows(v)], local.at[1])
    load_h.start()
    load_w = pltpu.make_async_copy(w_ref, w, local.at[0])
    load_w.start()

    pl.semaphore_wait(barrier, CUBE - 1 + n_dp - 1)

    low, high = pl.ds(0, half), pl.ds(half, half)
    x_low = push(h_ref.at[low], g.at[dev_rows(v, 0, half)], vocab=xp)
    y_high = push(h_ref.at[high], g.at[dev_rows(v, half, half)], vocab=yp)
    s_own = push(h_ref, g.at[dev_rows(v)], vocab=sib)
    for load in loads:
        load.wait()
    facts[v] = make_facts(*codes_in)
    facts_in = [push(facts.at[v], facts.at[v], vocab=peer) for peer in others]
    x_high = push(h_ref.at[high], g.at[dev_rows(v, half, half)], vocab=xp)
    y_low = push(h_ref.at[low], g.at[dev_rows(v, 0, half)], vocab=yp)
    far_in = []
    for m in far:
        columns = rows_at(groups[m] * part, part)
        far_in.append(push(h_ref.at[:, columns], parts.at[m - 2, v], dp=groups[m]))

    def forward(q, first, rows, **where):
        at = dev_rows(q, first, rows)
        return push(g.at[at], g.at[at], **where)

    wait(*facts_in)
    cand, only, own_place = read_facts(facts[...], v, visits, per_own)
    place[...] = own_place
    row = lax.broadcasted_iota(jnp.int32, (tokens, tokens), 0)
    lane = lax.broadcasted_iota(jnp.int32, (tokens, tokens), 1)
    eye = jnp.where(row == lane, 1.0, 0.0).astype(BF16)
    tile_row = lax.broadcasted_iota(jnp.int32, (TILE, tokens), 0)
    tile_lane = lax.broadcasted_iota(jnp.int32, (TILE, tokens), 1).astype(F32)
    for s in range(CUBE):
        both = jnp.concatenate([cand[s], only[s]], axis=0).astype(BF16)
        cols[s * tokens : (s + 1) * tokens, :] = lax.dot_general(
            eye, both, NT, preferred_element_type=F32
        )
        mine = jnp.where(tile_row == kinds, tile_lane, jnp.where(tile_row < kinds, only[s], 0.0))
        mine = jnp.concatenate([mine, jnp.zeros_like(mine)], axis=0).astype(BF16)
        ship[0, s] = lax.dot_general(
            mine, pick_of(place, s, kinds + 3, tokens), NT, preferred_element_type=F32
        ).astype(BF16)

    packs_in = {m: [] for m in range(1, n_dp)}

    def work(c, service=None):
        chip_scores(c, kinds, g, w, cols, grads, pk)
        near_columns = rows_at(groups[1] * part, part)
        for i in range(2):
            s = 2 * c + i
            pick = pick_of(place, s, kinds + 3, capacity)
            mine = pk[i * tokens : (i + 1) * tokens, :].astype(BF16)
            packed[0, s] = jnp.dot(pick, mine, preferred_element_type=F32).astype(BF16)
            near_out[rows_at(s * capacity, capacity), :] = jnp.dot(
                pick, g[dev_rows(s), near_columns], preferred_element_type=F32
            ).astype(BF16)
        two = pl.ds(2 * c, 2)
        for m in reversed(range(1, n_dp)):
            packs_in[m].append(push(packed.at[0, two], packed.at[m, two], dp=groups[m]))
            packs_in[m].append(push(ship.at[0, two], ship.at[m, two], dp=groups[m]))
        at = rows_at(2 * c * capacity, 2 * capacity)
        packs_in[1].append(push(near_out.at[at], near_in.at[at], dp=groups[1]))
        if service is not None:
            service()
        chip_back(c, count, w, grads, b)

    def pair(i, q):
        return push(b.at[dev_rows(flip(q, 1))], sbuf.at[i], vocab=sib)

    load_w.wait()
    load_h.wait()
    wait(s_own)
    work(chip)
    pair_own = pair(3, v)

    wait(x_low)
    d_low = forward(xp, 0, half, vocab=yp)
    s1 = forward(xp, 0, half, vocab=sib)
    wait(y_high)
    d_high = forward(yp, half, half, vocab=xp)
    s2 = forward(yp, half, half, vocab=sib)
    wait(x_high)
    s3 = forward(xp, half, half, vocab=sib)
    wait(y_low)
    s4 = forward(yp, 0, half, vocab=sib)
    wait(s1, s3)

    far_half = max(1, len(far) // 2)
    far_low, far_high = pl.ds(0, far_half), pl.ds(far_half, len(far) - far_half)
    far_copies = []

    def far_direct():
        wait(*far_in)
        for where in (dict(vocab=xp), dict(vocab=yp), dict(vocab=sib)):
            far_copies.append(push(parts.at[:, v], parts.at[:, v], **where))

    work(xc, far_direct)
    pair_x = pair(1, xp)
    wait(d_low)
    s5 = forward(diag, 0, half, vocab=sib)
    wait(d_high)
    s6 = forward(diag, half, half, vocab=sib)
    wait(s2, s4)

    def add_sum(i, q, first, hop=None):
        step = 16

        @pl.loop(0, half // step)
        def _(k):
            at = rows_at(first + k * step, step)
            total = b[rows_at(q * tokens + first + k * step, step), :].astype(F32)
            total = total + sbuf[i, at, :].astype(F32)
            if hop is not None:
                total = total + hop[rows_at(k * step, step), :].astype(F32)
            sums[i, at, :] = total.astype(BF16)

    back_copies = []

    def x_back():
        wait(pair_x)
        add_sum(1, xp, 0)
        back_copies.append(push(sums.at[1, low], fx.at[low], vocab=xp))

    work(yc, x_back)
    pair_y = pair(2, yp)
    wait(s5, s6)

    def y_back():
        wait(pair_y)
        add_sum(2, yp, half)
        back_copies.append(push(sums.at[2, high], fy.at[high], vocab=yp))

    work(dc, y_back)
    pair_d = pair(0, diag)
    wait(pair_d)
    add_sum(0, diag, 0)
    to_x = push(sums.at[0, low], hx, vocab=xp)
    add_sum(0, diag, half)
    to_y = push(sums.at[0, high], hy, vocab=yp)

    chunk = lhs_t.shape[1]
    own_columns = rows_at(dp * part, part)
    for i in range(CUBE * tokens // chunk):
        at = slice(i * chunk, (i + 1) * chunk)
        lhs_t[...] = g[at, own_columns].T
        add_product(lhs_t, lambda j, words_at, at=at: grads[at, words_at], acc, first=i == 0)

    wait(*far_copies)
    far_on = [
        push(parts.at[far_low, xp], parts.at[far_low, xp], vocab=yp),
        push(parts.at[far_high, yp], parts.at[far_high, yp], vocab=xp),
    ]
    far_sib = [push(parts.at[:, q], parts.at[:, q], vocab=sib) for q in (xp, yp)]

    token_lane = lax.broadcasted_iota(jnp.int32, (capacity, tokens), 1).astype(F32)

    def slot_codes(m):
        @pl.loop(0, CUBE)
        def _(s):
            only_cols[m - 1, rows_at(s * capacity, capacity), :] = lax.dot_general(
                eye[:capacity, :], ship[m, s], NT, preferred_element_type=F32
            )

    def compact(m, c):
        for i in range(2):
            s = 2 * c + i
            at = rows_at(s * capacity, capacity)
            token = only_cols[m - 1, at, kinds : kinds + 1]
            pick = jnp.where(jnp.broadcast_to(token, token_lane.shape) == token_lane, 1.0, 0.0)
            lhs[m - 2, at, :] = jnp.dot(
                pick.astype(BF16), parts[m - 2, s], preferred_element_type=F32
            ).astype(BF16)

    def other_product(m):
        lhs_t[...] = (near_in[...] if m == 1 else lhs[m - 2]).T

        def block_of(k):
            return packed[m, :, :, k * BLOCK : (k + 1) * BLOCK].reshape(CUBE * capacity, BLOCK)

        add_product(
            lhs_t,
            unpack(kinds, only_cols.at[m - 1], block_of),
            acc,
            out=wg_ref if m == n_dp - 1 else None,
        )

    for m in far:
        wait(*packs_in[m])
        slot_codes(m)
    wait(*far_sib)
    for m in far:
        for c in (chip, xc, yc):
            compact(m, c)
    wait(*packs_in[1])
    slot_codes(1)
    other_product(1)

    wait(to_y)
    add_sum(1, xp, half, hy)
    back_copies.append(push(sums.at[1, high], fx.at[high], vocab=xp))
    wait(to_x)
    add_sum(2, yp, 0, hx)
    back_copies.append(push(sums.at[2, low], fy.at[low], vocab=yp))

    wait(*far_on)
    far_last = [
        push(parts.at[far_low, diag], parts.at[far_low, diag], vocab=sib),
        push(parts.at[far_high, diag], parts.at[far_high, diag], vocab=sib),
    ]
    wait(*far_last)
    for m in far:
        compact(m, dc)
        other_product(m)

    wait(pair_own, *back_copies)
    step = 16

    @pl.loop(0, tokens // step)
    def _(k):
        at = rows_at(k * step, step)
        total = b[rows_at(v * tokens + k * step, step), :].astype(F32)
        total = total + sbuf[3, at, :].astype(F32)
        total = total + fx[at, :].astype(F32) + fy[at, :].astype(F32)
        o_ref[at, :] = total.astype(BF16)

    for copy in copies:
        copy.wait_send()


def cube_program(
    hidden, weight, owners, negatives, mask, block, word, norm, cot, n_dp, capacity
):
    tokens, width = hidden.shape
    words = weight.shape[1]
    visits, per_own = negatives.shape[1:]
    part = width // n_dp
    slots = CUBE * capacity
    group = CUBE * tokens
    kinds = per_own + 1
    vmem = pl.BlockSpec(memory_space=pltpu.VMEM)
    hbm = pl.BlockSpec(memory_space=pl.ANY)
    v = pltpu.VMEM
    total = 96
    return pl.pallas_call(
        lambda *refs: cube_kernel(n_dp, *refs),
        out_shape=(
            jax.ShapeDtypeStruct((tokens, width), BF16),
            jax.ShapeDtypeStruct((part, words), BF16),
        ),
        in_specs=[hbm] * 9,
        out_specs=(vmem, vmem),
        scratch_shapes=[
            v((visits, tokens), jnp.int32),
            v((visits, per_own, tokens), jnp.int32),
            v((visits, per_own, tokens), jnp.int32),
            v((1, tokens), jnp.int32),
            v((1, tokens), jnp.int32),
            v((1, tokens), BF16),
            v((1, tokens), BF16),
            v((width, words), BF16),
            v((group, width), BF16),
            v((group, width), BF16),
            v((4, tokens, width), BF16),
            v((3, tokens, width), BF16),
            v((tokens // 2, width), BF16),
            v((tokens // 2, width), BF16),
            v((tokens, width), BF16),
            v((tokens, width), BF16),
            v((CUBE, fact_rows(visits, per_own), tokens), BF16),
            v((CUBE, TILE, tokens), F32),
            v((n_dp, CUBE, 2 * TILE, tokens), BF16),
            v((group, 2 * TILE), F32),
            v((n_dp - 1, slots, 2 * TILE), F32),
            v((group, words), BF16),
            v((2 * tokens, kinds * BLOCK), F32),
            v((n_dp, CUBE, capacity, kinds * BLOCK), BF16),
            v((n_dp - 2, CUBE, tokens, part), BF16),
            v((slots, part), BF16),
            v((slots, part), BF16),
            v((n_dp - 2, slots, part), BF16),
            v((part, slots), BF16),
            v((part, words), F32),
            pltpu.SemaphoreType.DMA((total,)),
            pltpu.SemaphoreType.DMA((total,)),
            pltpu.SemaphoreType.DMA((9,)),
        ],
        compiler_params=pltpu.CompilerParams(
            collective_id=0, has_side_effects=True, vmem_limit_bytes=62 * 2**20
        ),
        name="cube",
    )(
        hidden,
        weight,
        owners.T,
        jnp.transpose(negatives, (1, 2, 0)),
        jnp.transpose(mask, (1, 2, 0)),
        block[None, :],
        word[None, :],
        norm[None, :],
        cot[None, :],
    )


def weight_kernel(own_ref, pick_ref, part_ref, packed_ref, only_ref, o_ref, lhs, lhs_t, acc):
    g = pl.program_id(0)
    sources, capacity = pick_ref.shape[:2]
    kinds = only_ref.shape[1]
    pair = 2 * BLOCK

    @pl.when(g == 0)
    def _():
        lhs[...] = own_ref[...]
        acc[...] = jnp.zeros_like(acc)

    @pl.when(g > 0)
    def _():
        for s in range(sources):
            lhs[s * capacity : (s + 1) * capacity, :] = jnp.dot(
                pick_ref[s], part_ref[0, s], preferred_element_type=F32
            ).astype(BF16)

    lhs_t[...] = lhs[...].T

    @pl.loop(0, acc.shape[1] // pair, unroll=True)
    def _(j):
        sides = []
        for i in range(2):
            block = (2 * j + i + 1).astype(F32)
            value = jnp.zeros((lhs.shape[0], BLOCK), F32)
            for k in range(kinds):
                value = jnp.where(
                    only_ref[:, k : k + 1] == block,
                    packed_ref[0, :, k * BLOCK : (k + 1) * BLOCK].astype(F32),
                    value,
                )
            sides.append(value.astype(BF16))
        spread = jnp.concatenate(sides, axis=1)
        at = pl.ds(pl.multiple_of(j * pair, pair), pair)
        acc[:, at] += jnp.dot(lhs_t[...], spread, preferred_element_type=F32)

    @pl.when(g == pl.num_programs(0) - 1)
    def _():
        o_ref[...] = acc[...].astype(BF16)


def weight_product(own, pick, parts, packed, only, words):
    groups, slots = packed.shape[:2]
    _, sources, tokens, part = parts.shape
    capacity = pick.shape[1]
    kinds = only.shape[1]
    return pl.pallas_call(
        weight_kernel,
        grid=(groups,),
        out_shape=jax.ShapeDtypeStruct((part, words), BF16),
        in_specs=[
            pl.BlockSpec((slots, part), lambda g: (0, 0)),
            pl.BlockSpec((sources, capacity, tokens), lambda g: (jnp.maximum(g - 1, 0), 0, 0)),
            pl.BlockSpec((1, sources, tokens, part), lambda g: (jnp.maximum(g - 1, 0), 0, 0, 0)),
            pl.BlockSpec((1, slots, packed.shape[2]), lambda g: (g, 0, 0)),
            pl.BlockSpec((slots, kinds), lambda g: (g, 0)),
        ],
        out_specs=pl.BlockSpec((part, words), lambda g: (0, 0)),
        scratch_shapes=[
            pltpu.VMEM((slots, part), BF16),
            pltpu.VMEM((part, slots), BF16),
            pltpu.VMEM((part, words), F32),
        ],
        compiler_params=pltpu.CompilerParams(dimension_semantics=("arbitrary",)),
        name="weight_product",
    )(own, pick, parts, packed, only)


def body(
    hidden,
    output_weight,
    owners,
    negatives,
    negative_mask,
    target_block,
    target_word,
    log_norm,
    cotangent,
):
    tokens, width = hidden.shape
    visits = owners.shape[1]
    per_own = negatives.shape[2]
    n_vocab = lax.axis_size("vocab")
    n_dp = lax.axis_size("dp")
    me = lax.axis_index("vocab")
    my_dp = lax.axis_index("dp")
    words = output_weight.shape[1]
    capacity = max(2, tokens * visits * 4 // (3 * n_vocab))
    if n_vocab == CUBE and n_dp == LINE:
        return cube_program(
            hidden,
            output_weight,
            owners,
            negatives,
            negative_mask,
            target_block,
            target_word,
            log_norm,
            cotangent,
            n_dp,
            capacity,
        )
    slots = n_vocab * capacity
    part = width // n_dp

    facts = jnp.concatenate(
        [
            owners.T,
            negatives.reshape(tokens, -1).T,
            negative_mask.reshape(tokens, -1).T,
            target_block[None, :],
            target_word[None, :],
        ],
        axis=0,
    ).astype(BF16)
    facts = jnp.concatenate([facts, log_norm[None, :], cotangent[None, :]], axis=0)
    facts = jnp.pad(facts, ((0, -facts.shape[0] % 16), (0, 0)))
    blocks = n_dp * n_vocab

    group_rows = lax.all_gather(hidden, "vocab", axis=0, tiled=False)
    part_rows = lax.all_to_all(hidden, "dp", split_axis=1, concat_axis=0, tiled=True)
    part_rows = jnp.roll(part_rows.reshape(n_dp, tokens, part), -my_dp, axis=0)[1:]
    facts = lax.all_gather(lax.all_gather(facts, "dp", axis=0), "vocab", axis=0)
    facts = jnp.roll(facts, -my_dp, axis=1)
    part_rows = lax.all_gather(part_rows, "vocab", axis=1)
    facts = jnp.swapaxes(facts, 0, 1).reshape(blocks, -1, tokens)

    f = facts.astype(F32)
    pairs = visits * per_own
    hit = f[:, :visits, :] == me.astype(F32)
    neg = f[:, visits : visits + pairs, :]
    mask = f[:, visits + pairs : visits + 2 * pairs, :]
    base = visits + 2 * pairs
    t_block, t_word, norm, cot = (f[:, base + i, :] for i in range(4))
    named = jnp.any(hit, axis=1)
    cand = [jnp.where(hit[:, 0], t_block + 1.0, 0.0)]
    for n in range(per_own):
        value = jnp.zeros_like(t_block)
        for v in range(visits):
            i = v * per_own + n
            value = jnp.where(hit[:, v] & (mask[:, i] == 1.0), neg[:, i] + 1.0, value)
        cand.append(value)
    only = []
    for k, value in enumerate(cand):
        for earlier in cand[:k]:
            value = jnp.where(value == earlier, 0.0, value)
        only.append(value)
    upper = jnp.triu(jnp.ones((tokens, tokens), BF16), 1)
    rank = jnp.dot(named.astype(BF16), upper, preferred_element_type=F32)
    place = jnp.where(named, rank, -1.0)
    pick = (
        place[:, None, :] == jnp.arange(capacity, dtype=jnp.int32).astype(F32)[None, :, None]
    ).astype(BF16)
    attrs = jnp.stack(cand + only + [t_word, norm, cot], axis=1).astype(BF16)
    slot_facts = jnp.einsum("sct,sat->sca", pick, attrs, preferred_element_type=F32)
    kinds = per_own + 1
    all_only = slot_facts[:, :, kinds : 2 * kinds].reshape(n_dp * slots, kinds)
    mine = slot_facts[:n_vocab].reshape(slots, -1)
    my_pick = pick[:n_vocab]

    rows = jnp.einsum("sct,sth->sch", my_pick, group_rows, preferred_element_type=F32)
    rows = rows.astype(BF16).reshape(slots, width)
    scores = jnp.dot(rows, output_weight, preferred_element_type=F32)
    word_ids = jnp.arange(words, dtype=jnp.int32)[None, :]
    word_block = (word_ids // BLOCK + 1).astype(F32)
    word_in = (word_ids % BLOCK).astype(F32)
    counts = jnp.zeros((slots, words), F32)
    for k in range(kinds):
        counts = counts + jnp.where(mine[:, k : k + 1] == word_block, 1.0, 0.0)
    hot = jnp.where(
        (mine[:, 0:1] == word_block) & (mine[:, 2 * kinds : 2 * kinds + 1] == word_in), 1.0, 0.0
    )
    norm_col = mine[:, 2 * kinds + 1 : 2 * kinds + 2]
    cot_col = mine[:, 2 * kinds + 2 : 2 * kinds + 3]
    grown = jnp.where(counts > 0.0, counts * jnp.exp(scores - norm_col), 0.0)
    grad = (cot_col * (grown - hot)).astype(BF16)

    packed = []
    for k in range(kinds):
        which = mine[:, kinds + k : kinds + k + 1]
        value = jnp.zeros((slots, BLOCK), BF16)
        for b in range(BLK_DEV):
            value = jnp.where(which == b + 1.0, grad[:, b * BLOCK : (b + 1) * BLOCK], value)
        packed.append(value)
    packed = jnp.concatenate(packed, axis=1)
    back = lax.dot_general(
        grad, output_weight, (((1,), (1,)), ((), ())), preferred_element_type=F32
    ).astype(BF16)
    back = jnp.einsum(
        "sct,sch->sth", my_pick, back.reshape(n_vocab, capacity, width), preferred_element_type=F32
    ).astype(BF16)
    hidden_grad = lax.psum_scatter(
        back.reshape(n_vocab * tokens, width), "vocab", scatter_dimension=0, tiled=True
    )
    packed = jnp.roll(lax.all_gather(packed, "dp", axis=0), -my_dp, axis=0)
    own_slots = lax.dynamic_slice_in_dim(rows, my_dp * part, part, 1)
    weight_grad = weight_product(own_slots, pick[n_vocab:], part_rows, packed, all_only, words)
    return (hidden_grad, weight_grad)


def solution(mesh):
    placed = (
        P(("dp", "vocab"), None),
        P(None, "vocab"),
        P(("dp", "vocab"), None),
        P(("dp", "vocab"), None, None),
        P(("dp", "vocab"), None, None),
        P(("dp", "vocab")),
        P(("dp", "vocab")),
        P(("dp", "vocab")),
        P(("dp", "vocab")),
    )
    return jax.shard_map(
        body,
        mesh=mesh,
        in_specs=placed,
        out_specs=(P(("dp", "vocab"), None), P("dp", "vocab")),
        check_vma=False,
    )
```

```python
import jax
import jax.numpy as jnp
from jax import lax
from jax.experimental import pallas as pl
from jax.experimental.pallas import tpu as pltpu
from jax.sharding import PartitionSpec as P

BLOCK = 128
BLK_DEV = 8
F32 = jnp.float32
BF16 = jnp.bfloat16


MESH = pl.DeviceIdType.MESH
CUBE = 8
LINE = 4
PIECES = 2
TILE = 8
NT = (((1,), (1,)), ((), ()))


def rows_at(start, count):
    return pl.ds(pl.multiple_of(start, count), count)


def make_facts(own_ref, neg_ref, mask_ref, block_ref, word_ref, norm_ref, cot_ref):
    visits, tokens = own_ref.shape
    per_own = neg_ref.shape[1]
    code = jnp.where(mask_ref[...] == 1, neg_ref[...] + 1, 0).astype(F32)
    owners = own_ref[...].astype(F32)
    lines = [owners[v : v + 1, :] for v in range(visits)] + [block_ref[...].astype(F32) + 1.0]
    lines += [code[v, n : n + 1, :] for v in range(visits) for n in range(per_own)]
    lines += [ref[...].astype(F32) for ref in (word_ref, norm_ref, cot_ref)]
    count = fact_rows(visits, per_own)
    row = lax.broadcasted_iota(jnp.int32, (count, tokens), 0)
    tile = jnp.zeros((count, tokens), F32)
    for i, line in enumerate(lines):
        tile = jnp.where(row == i, jnp.broadcast_to(line, (count, tokens)), tile)
    return tile.astype(BF16)


def fact_rows(visits, per_own):
    rows = visits * (1 + per_own) + 4
    return rows + -rows % (2 * TILE)


def read_facts(facts, me, visits, per_own):
    f = facts.astype(F32)
    sources, _, tokens = f.shape
    kinds = per_own + 1
    line = lambda i: f[:, i : i + 1, :]
    hit = [jnp.where(line(v) == me.astype(F32), 1.0, 0.0) for v in range(visits)]
    named = sum(hit[1:], hit[0])
    lines = [hit[0] * line(visits)]
    for n in range(per_own):
        terms = [hit[v] * line(visits + 1 + v * per_own + n) for v in range(visits)]
        lines.append(sum(terms[1:], terms[0]))
    base = visits + 1 + visits * per_own
    lines += [named * line(base + i) for i in range(3)] + [named]
    row = lax.broadcasted_iota(jnp.int32, (sources, TILE, tokens), 1)
    cand = jnp.zeros((sources, TILE, tokens), F32)
    for i, value in enumerate(lines):
        cand = jnp.where(row == i, jnp.broadcast_to(value, cand.shape), cand)
    only = cand
    for k in range(kinds - 1):
        earlier = jnp.broadcast_to(lines[k], cand.shape)
        only = jnp.where((row > k) & (row < kinds) & (cand == earlier), 0.0, only)
    before = lax.broadcasted_iota(jnp.int32, (tokens, tokens), 0)
    after = lax.broadcasted_iota(jnp.int32, (tokens, tokens), 1)
    upper = jnp.where(before < after, 1.0, 0.0).astype(BF16)
    flat = cand.reshape(sources * TILE, tokens).astype(BF16)
    rank = jnp.dot(flat, upper, preferred_element_type=F32).reshape(cand.shape)
    place = jnp.where(cand > 0.0, rank, -1.0)
    return cand, only, place


def pick_of(place_ref, s, line, slots):
    tokens = place_ref.shape[2]
    place = place_ref[s][line : line + 1, :]
    slot = lax.broadcasted_iota(jnp.int32, (slots, tokens), 0).astype(F32)
    return jnp.where(jnp.broadcast_to(place, (slots, tokens)) == slot, 1.0, 0.0).astype(BF16)


def chip_scores(c, kinds, g, w, cols, grads, pk):
    count = pk.shape[0]
    words = w.shape[1]
    pair = 2 * BLOCK
    at = rows_at(c * count, count)
    lane = lax.broadcasted_iota(jnp.int32, (count, BLOCK), 1).astype(F32)
    pk[...] = jnp.zeros_like(pk)

    @pl.loop(0, words // pair)
    def _(j):
        words_at = rows_at(j * pair, pair)
        scores = jnp.dot(g[at, :], w[:, words_at], preferred_element_type=F32)
        col = [jnp.broadcast_to(cols[at, i : i + 1], (count, BLOCK)) for i in range(kinds + 3)]
        only = [
            jnp.broadcast_to(cols[at, TILE + i : TILE + i + 1], (count, BLOCK))
            for i in range(kinds)
        ]
        word, norm, cot = col[kinds:]
        here = jnp.where(word == lane, 1.0, 0.0)
        sides = []
        for i in range(2):
            block = (2 * j + i + 1).astype(F32)
            counts = jnp.where(col[0] == block, 1.0, 0.0)
            hot = counts * here
            for k in range(1, kinds):
                counts = counts + jnp.where(col[k] == block, 1.0, 0.0)
            score = scores[:, i * BLOCK : (i + 1) * BLOCK]
            grown = jnp.where(counts > 0.0, counts * jnp.exp(score - norm), 0.0)
            grad = cot * (grown - hot)
            for k in range(kinds):
                spot = slice(k * BLOCK, (k + 1) * BLOCK)
                pk[:, spot] = jnp.where(only[k] == block, grad, pk[:, spot])
            sides.append(grad.astype(BF16))
        grads[at, words_at] = jnp.concatenate(sides, axis=1)


def chip_back(c, count, w, grads, b):
    width = w.shape[0]
    step = min(512, width)
    at = rows_at(c * count, count)

    @pl.loop(0, width // step)
    def _(j):
        cut = rows_at(j * step, step)
        b[at, cut] = lax.dot_general(
            grads[at, :], w[cut, :], NT, preferred_element_type=F32
        ).astype(BF16)


def add_product(lhs_t, spread, acc, out=None, first=False):
    pair = 2 * BLOCK

    @pl.loop(0, acc.shape[1] // pair)
    def _(j):
        at = rows_at(j * pair, pair)
        value = jnp.dot(lhs_t[...], spread(j, at), preferred_element_type=F32)
        if not first:
            value = value + acc[:, at]
        if out is None:
            acc[:, at] = value
        else:
            out[:, at] = value.astype(BF16)


def unpack(kinds, only_cols, packed):
    def spread(j, _):
        sides = []
        for i in range(2):
            block = (2 * j + i + 1).astype(F32)
            value = None
            for k in range(kinds):
                mine = jnp.broadcast_to(only_cols[:, k : k + 1], (only_cols.shape[0], BLOCK)) == block
                term = packed(k).astype(F32)
                value = jnp.where(mine, term, 0.0 if value is None else value)
            sides.append(value.astype(BF16))
        return jnp.concatenate(sides, axis=1)

    return spread


def flip(value, m):
    bit, out = 1, value
    while bit <= m:
        if m & bit:
            out = out + bit - 2 * bit * ((value // bit) % 2)
        bit *= 2
    return out


def cube_kernel(
    n_dp,
    h_ref,
    w_ref,
    own_ref,
    neg_ref,
    mask_ref,
    block_ref,
    word_ref,
    norm_ref,
    cot_ref,
    mine_ref,
    fx_ref,
    fy_ref,
    wg_ref,
    own_in,
    neg_in,
    mask_in,
    block_in,
    word_in,
    norm_in,
    cot_in,
    w,
    g,
    b,
    sbuf,
    sums,
    own_sum,
    hx,
    hy,
    wg,
    facts,
    place,
    ship,
    cols,
    only_cols,
    grads,
    pk,
    packed,
    parts,
    near_out,
    near_in,
    lhs,
    lhs_t,
    acc,
    send,
    recv,
    local,
):
    v = lax.axis_index("vocab")
    dp = lax.axis_index("dp")
    sib, xp, yp = flip(v, 1), flip(v, 2), flip(v, 4)
    diag = flip(v, 6)
    chip, xc, yc, dc = v // 2, xp // 2, yp // 2, diag // 2
    tokens, width = h_ref.shape
    visits, per_own = neg_in.shape[:2]
    kinds = per_own + 1
    part = width // n_dp
    half = tokens // 2
    capacity = packed.shape[2]
    count = 2 * tokens
    others = [flip(v, u) for u in range(1, CUBE)]
    groups = [flip(dp, m) for m in range(n_dp)]
    far = range(2, n_dp)
    copies = []

    barrier = pltpu.get_barrier_semaphore()
    for peer in others:
        pl.semaphore_signal(barrier, inc=1, device_id={"vocab": peer}, device_id_type=MESH)
    for peer in groups[1:]:
        pl.semaphore_signal(barrier, inc=1, device_id={"dp": peer}, device_id_type=MESH)

    def push(src, dst, **where):
        i = len(copies)
        copy = pltpu.make_async_remote_copy(
            src_ref=src,
            dst_ref=dst,
            send_sem=send.at[i],
            recv_sem=recv.at[i],
            device_id=where,
            device_id_type=MESH,
        )
        copy.start()
        copies.append(copy)
        return copy

    def wait(*items):
        for copy in items:
            copy.wait_recv()

    def dev_rows(q, first=0, rows=None):
        rows = tokens if rows is None else rows
        return rows_at(q * tokens + first, rows)

    codes_in = (own_in, neg_in, mask_in, block_in, word_in, norm_in, cot_in)
    loads = []
    for i, (src, dst) in enumerate(
        zip(
            (own_ref, neg_ref, mask_ref, block_ref, word_ref, norm_ref, cot_ref),
            codes_in,
        )
    ):
        loads.append(pltpu.make_async_copy(src, dst, local.at[2 + i]))
        loads[-1].start()
    load_h = pltpu.make_async_copy(h_ref, g.at[dev_rows(v)], local.at[1])
    load_h.start()
    load_w = pltpu.make_async_copy(w_ref, w, local.at[0])
    load_w.start()

    pl.semaphore_wait(barrier, CUBE - 1 + n_dp - 1)

    low, high = pl.ds(0, half), pl.ds(half, half)
    x_low = push(h_ref.at[low], g.at[dev_rows(v, 0, half)], vocab=xp)
    y_high = push(h_ref.at[high], g.at[dev_rows(v, half, half)], vocab=yp)
    s_own = push(h_ref, g.at[dev_rows(v)], vocab=sib)
    for load in loads:
        load.wait()
    facts[v] = make_facts(*codes_in)
    facts_in = [push(facts.at[v], facts.at[v], vocab=peer) for peer in others]
    x_high = push(h_ref.at[high], g.at[dev_rows(v, half, half)], vocab=xp)
    y_low = push(h_ref.at[low], g.at[dev_rows(v, 0, half)], vocab=yp)
    far_in = []
    for m in far:
        columns = rows_at(groups[m] * part, part)
        far_in.append(push(h_ref.at[:, columns], parts.at[m - 2, v], dp=groups[m]))

    def forward(q, first, rows, **where):
        at = dev_rows(q, first, rows)
        return push(g.at[at], g.at[at], **where)

    wait(*facts_in)
    cand, only, own_place = read_facts(facts[...], v, visits, per_own)
    place[...] = own_place
    row = lax.broadcasted_iota(jnp.int32, (tokens, tokens), 0)
    lane = lax.broadcasted_iota(jnp.int32, (tokens, tokens), 1)
    eye = jnp.where(row == lane, 1.0, 0.0).astype(BF16)
    tile_row = lax.broadcasted_iota(jnp.int32, (TILE, tokens), 0)
    tile_lane = lax.broadcasted_iota(jnp.int32, (TILE, tokens), 1).astype(F32)
    for s in range(CUBE):
        both = jnp.concatenate([cand[s], only[s]], axis=0).astype(BF16)
        cols[s * tokens : (s + 1) * tokens, :] = lax.dot_general(
            eye, both, NT, preferred_element_type=F32
        )
        mine = jnp.where(tile_row == kinds, tile_lane, jnp.where(tile_row < kinds, only[s], 0.0))
        mine = jnp.concatenate([mine, jnp.zeros_like(mine)], axis=0).astype(BF16)
        ship[0, s] = lax.dot_general(
            mine, pick_of(place, s, kinds + 3, tokens), NT, preferred_element_type=F32
        ).astype(BF16)

    packs_in = {m: [] for m in range(1, n_dp)}

    def work(c, service=None):
        chip_scores(c, kinds, g, w, cols, grads, pk)
        near_columns = rows_at(groups[1] * part, part)
        for i in range(2):
            s = 2 * c + i
            pick = pick_of(place, s, kinds + 3, capacity)
            mine = pk[i * tokens : (i + 1) * tokens, :].astype(BF16)
            packed[0, s] = jnp.dot(pick, mine, preferred_element_type=F32).astype(BF16)
            near_out[rows_at(s * capacity, capacity), :] = jnp.dot(
                pick, g[dev_rows(s), near_columns], preferred_element_type=F32
            ).astype(BF16)
        two = pl.ds(2 * c, 2)
        for m in reversed(range(1, n_dp)):
            packs_in[m].append(push(packed.at[0, two], packed.at[m, two], dp=groups[m]))
            packs_in[m].append(push(ship.at[0, two], ship.at[m, two], dp=groups[m]))
        at = rows_at(2 * c * capacity, 2 * capacity)
        packs_in[1].append(push(near_out.at[at], near_in.at[at], dp=groups[1]))
        if service is not None:
            service()
        chip_back(c, count, w, grads, b)

    def pair(i, q):
        return push(b.at[dev_rows(flip(q, 1))], sbuf.at[i], vocab=sib)

    load_w.wait()
    load_h.wait()
    wait(s_own)
    work(chip)
    pair_own = pair(3, v)

    wait(x_low)
    d_low = forward(xp, 0, half, vocab=yp)
    s1 = forward(xp, 0, half, vocab=sib)
    wait(y_high)
    d_high = forward(yp, half, half, vocab=xp)
    s2 = forward(yp, half, half, vocab=sib)
    wait(x_high)
    s3 = forward(xp, half, half, vocab=sib)
    wait(y_low)
    s4 = forward(yp, 0, half, vocab=sib)
    wait(s1, s3)

    far_half = max(1, len(far) // 2)
    far_low, far_high = pl.ds(0, far_half), pl.ds(far_half, len(far) - far_half)
    far_copies = []

    def far_direct():
        wait(*far_in)
        for where in (dict(vocab=xp), dict(vocab=yp), dict(vocab=sib)):
            far_copies.append(push(parts.at[:, v], parts.at[:, v], **where))

    def add_sum(i, q, first, rows, hop=None, hop_first=0):
        step = 16

        @pl.loop(0, rows // step)
        def _(k):
            at = rows_at(first + k * step, step)
            total = b[rows_at(q * tokens + first + k * step, step), :].astype(F32)
            total = total + sbuf[i, at, :].astype(F32)
            if hop is not None:
                total = total + hop[rows_at(hop_first + k * step, step), :].astype(F32)
            sums[i, at, :] = total.astype(BF16)

    back_copies = []
    from_diag = []

    def during_y():
        wait(d_low)
        from_diag.append(forward(diag, 0, half, vocab=sib))
        wait(d_high)
        from_diag.append(forward(diag, half, half, vocab=sib))
        wait(pair_x)
        add_sum(1, xp, 0, half)
        back_copies.append(push(sums.at[1, low], fx_ref.at[low], vocab=xp))

    def y_back():
        wait(pair_y)
        add_sum(2, yp, half, half)
        back_copies.append(push(sums.at[2, high], fy_ref.at[high], vocab=yp))

    work(xc, far_direct)
    pair_x = pair(1, xp)
    wait(s2, s4)
    work(yc, during_y)
    pair_y = pair(2, yp)
    wait(*from_diag)
    y_back()
    work(dc)
    pair_d = pair(0, diag)
    wait(pair_d)
    piece = half // PIECES
    to_x, to_y = [], []
    for i in range(PIECES):
        add_sum(0, diag, i * piece, piece)
        to_x.append(
            push(sums.at[0, pl.ds(i * piece, piece)], hx.at[pl.ds(i * piece, piece)], vocab=xp)
        )
        add_sum(0, diag, half + i * piece, piece)
        to_y.append(
            push(
                sums.at[0, pl.ds(half + i * piece, piece)],
                hy.at[pl.ds(i * piece, piece)],
                vocab=yp,
            )
        )

    def hops(i):
        at = pl.ds(i * piece, piece)
        wait(to_x[i])
        add_sum(2, yp, i * piece, piece, hx, i * piece)
        back_copies.append(push(sums.at[2, at], fy_ref.at[at], vocab=yp))
        at = pl.ds(half + i * piece, piece)
        wait(to_y[i])
        add_sum(1, xp, half + i * piece, piece, hy, i * piece)
        back_copies.append(push(sums.at[1, at], fx_ref.at[at], vocab=xp))

    wait(pair_own)
    step = 16

    @pl.loop(0, tokens // step)
    def _(k):
        at = rows_at(k * step, step)
        total = b[rows_at(v * tokens + k * step, step), :].astype(F32)
        own_sum[at, :] = (total + sbuf[3, at, :].astype(F32)).astype(BF16)

    keep_mine = pltpu.make_async_copy(own_sum, mine_ref, local.at[1])
    keep_mine.start()

    chunk = lhs_t.shape[1]
    own_columns = rows_at(dp * part, part)
    for i in range(CUBE * tokens // chunk):
        at = slice(i * chunk, (i + 1) * chunk)
        lhs_t[...] = g[at, own_columns].T
        add_product(lhs_t, lambda j, words_at, at=at: grads[at, words_at], acc, first=i == 0)

    wait(*far_copies)
    far_on = [
        push(parts.at[far_low, xp], parts.at[far_low, xp], vocab=yp),
        push(parts.at[far_high, yp], parts.at[far_high, yp], vocab=xp),
    ]
    far_sib = [push(parts.at[:, q], parts.at[:, q], vocab=sib) for q in (xp, yp)]

    token_lane = lax.broadcasted_iota(jnp.int32, (capacity, tokens), 1).astype(F32)

    def slot_codes(m):
        @pl.loop(0, CUBE)
        def _(s):
            only_cols[m - 1, rows_at(s * capacity, capacity), :] = lax.dot_general(
                eye[:capacity, :], ship[m, s], NT, preferred_element_type=F32
            )

    def compact(m, c):
        for i in range(2):
            s = 2 * c + i
            at = rows_at(s * capacity, capacity)
            token = only_cols[m - 1, at, kinds : kinds + 1]
            pick = jnp.where(jnp.broadcast_to(token, token_lane.shape) == token_lane, 1.0, 0.0)
            lhs[m - 2, at, :] = jnp.dot(
                pick.astype(BF16), parts[m - 2, s], preferred_element_type=F32
            ).astype(BF16)

    def other_product(m):
        lhs_t[...] = (near_in[...] if m == 1 else lhs[m - 2]).T

        def block_of(k):
            return packed[m, :, :, k * BLOCK : (k + 1) * BLOCK].reshape(CUBE * capacity, BLOCK)

        add_product(
            lhs_t,
            unpack(kinds, only_cols.at[m - 1], block_of),
            acc,
            out=wg if m == n_dp - 1 else None,
        )

    for m in far:
        wait(*packs_in[m])
        slot_codes(m)
    wait(*far_sib)
    for m in far:
        for c in (chip, xc, yc):
            compact(m, c)
    for i in range(PIECES):
        hops(i)
    wait(*packs_in[1])
    slot_codes(1)
    other_product(1)
    wait(*far_on)
    far_last = [
        push(parts.at[far_low, diag], parts.at[far_low, diag], vocab=sib),
        push(parts.at[far_high, diag], parts.at[far_high, diag], vocab=sib),
    ]
    wait(*far_last)
    for m in far:
        compact(m, dc)
        other_product(m)

    keep_wg = pltpu.make_async_copy(wg, wg_ref, local.at[0])
    keep_wg.start()
    keep_mine.wait()
    keep_wg.wait()
    wait(*back_copies)
    for copy in copies:
        copy.wait_send()


def cube_program(
    hidden, weight, owners, negatives, mask, block, word, norm, cot, n_dp, capacity
):
    tokens, width = hidden.shape
    words = weight.shape[1]
    visits, per_own = negatives.shape[1:]
    part = width // n_dp
    slots = CUBE * capacity
    group = CUBE * tokens
    kinds = per_own + 1
    hbm = pl.BlockSpec(memory_space=pl.ANY)
    v = pltpu.VMEM
    total = 96
    state = jax.ShapeDtypeStruct((tokens, width), BF16)
    terms = pl.pallas_call(
        lambda *refs: cube_kernel(n_dp, *refs),
        out_shape=(state, state, state, jax.ShapeDtypeStruct((part, words), BF16)),
        in_specs=[hbm] * 9,
        out_specs=(hbm,) * 4,
        scratch_shapes=[
            v((visits, tokens), jnp.int32),
            v((visits, per_own, tokens), jnp.int32),
            v((visits, per_own, tokens), jnp.int32),
            v((1, tokens), jnp.int32),
            v((1, tokens), jnp.int32),
            v((1, tokens), BF16),
            v((1, tokens), BF16),
            v((width, words), BF16),
            v((group, width), BF16),
            v((group, width), BF16),
            v((4, tokens, width), BF16),
            v((3, tokens, width), BF16),
            v((tokens, width), BF16),
            v((tokens // 2, width), BF16),
            v((tokens // 2, width), BF16),
            v((part, words), BF16),
            v((CUBE, fact_rows(visits, per_own), tokens), BF16),
            v((CUBE, TILE, tokens), F32),
            v((n_dp, CUBE, 2 * TILE, tokens), BF16),
            v((group, 2 * TILE), F32),
            v((n_dp - 1, slots, 2 * TILE), F32),
            v((group, words), BF16),
            v((2 * tokens, kinds * BLOCK), F32),
            v((n_dp, CUBE, capacity, kinds * BLOCK), BF16),
            v((n_dp - 2, CUBE, tokens, part), BF16),
            v((slots, part), BF16),
            v((slots, part), BF16),
            v((n_dp - 2, slots, part), BF16),
            v((part, slots), BF16),
            v((part, words), F32),
            pltpu.SemaphoreType.DMA((total,)),
            pltpu.SemaphoreType.DMA((total,)),
            pltpu.SemaphoreType.DMA((9,)),
        ],
        compiler_params=pltpu.CompilerParams(
            collective_id=0, has_side_effects=True, vmem_limit_bytes=62 * 2**20
        ),
        name="cube",
    )(
        hidden,
        weight,
        owners.T,
        jnp.transpose(negatives, (1, 2, 0)),
        jnp.transpose(mask, (1, 2, 0)),
        block[None, :],
        word[None, :],
        norm[None, :],
        cot[None, :],
    )
    return finish(*terms)


def finish_kernel(a_ref, b_ref, c_ref, wg_ref, o_ref, out_ref, a, b, c, o, wg, sems):
    pieces = 4
    rows, deep = a.shape[0] // pieces, wg.shape[0] // pieces
    loads, stores = [], []

    def start(src, dst, i):
        copy = pltpu.make_async_copy(src, dst, sems.at[i])
        copy.start()
        return copy

    cuts = [pl.ds(i * rows, rows) for i in range(pieces)]
    deep_cuts = [pl.ds(i * deep, deep) for i in range(pieces)]
    for i, at in enumerate(cuts):
        loads.append(
            [
                start(src.at[at], dst.at[at], 3 * i + k)
                for k, (src, dst) in enumerate(((a_ref, a), (b_ref, b), (c_ref, c)))
            ]
        )
    deep_loads = [
        start(wg_ref.at[at], wg.at[at], 3 * pieces + i) for i, at in enumerate(deep_cuts)
    ]
    for i, at in enumerate(cuts):
        for copy in loads[i]:
            copy.wait()
        total = a[at, :].astype(F32) + b[at, :].astype(F32) + c[at, :].astype(F32)
        o[at, :] = total.astype(BF16)
        stores.append(start(o.at[at], o_ref.at[at], 4 * pieces + i))
    for i, at in enumerate(deep_cuts):
        deep_loads[i].wait()
        stores.append(start(wg.at[at], out_ref.at[at], 5 * pieces + i))
    for copy in stores:
        copy.wait()


def finish(mine, fx, fy, weight):
    hbm = pl.BlockSpec(memory_space=pl.ANY)
    like = lambda x: jax.ShapeDtypeStruct(x.shape, x.dtype)
    v = pltpu.VMEM
    return pl.pallas_call(
        finish_kernel,
        out_shape=(like(mine), like(weight)),
        in_specs=[hbm] * 4,
        out_specs=(hbm,) * 2,
        scratch_shapes=[v(mine.shape, BF16)] * 4
        + [v(weight.shape, BF16), pltpu.SemaphoreType.DMA((24,))],
        compiler_params=pltpu.CompilerParams(vmem_limit_bytes=60 * 2**20),
        name="finish",
    )(mine, fx, fy, weight)


def weight_kernel(own_ref, pick_ref, part_ref, packed_ref, only_ref, o_ref, lhs, lhs_t, acc):
    g = pl.program_id(0)
    sources, capacity = pick_ref.shape[:2]
    kinds = only_ref.shape[1]
    pair = 2 * BLOCK

    @pl.when(g == 0)
    def _():
        lhs[...] = own_ref[...]
        acc[...] = jnp.zeros_like(acc)

    @pl.when(g > 0)
    def _():
        for s in range(sources):
            lhs[s * capacity : (s + 1) * capacity, :] = jnp.dot(
                pick_ref[s], part_ref[0, s], preferred_element_type=F32
            ).astype(BF16)

    lhs_t[...] = lhs[...].T

    @pl.loop(0, acc.shape[1] // pair, unroll=True)
    def _(j):
        sides = []
        for i in range(2):
            block = (2 * j + i + 1).astype(F32)
            value = jnp.zeros((lhs.shape[0], BLOCK), F32)
            for k in range(kinds):
                value = jnp.where(
                    only_ref[:, k : k + 1] == block,
                    packed_ref[0, :, k * BLOCK : (k + 1) * BLOCK].astype(F32),
                    value,
                )
            sides.append(value.astype(BF16))
        spread = jnp.concatenate(sides, axis=1)
        at = pl.ds(pl.multiple_of(j * pair, pair), pair)
        acc[:, at] += jnp.dot(lhs_t[...], spread, preferred_element_type=F32)

    @pl.when(g == pl.num_programs(0) - 1)
    def _():
        o_ref[...] = acc[...].astype(BF16)


def weight_product(own, pick, parts, packed, only, words):
    groups, slots = packed.shape[:2]
    _, sources, tokens, part = parts.shape
    capacity = pick.shape[1]
    kinds = only.shape[1]
    return pl.pallas_call(
        weight_kernel,
        grid=(groups,),
        out_shape=jax.ShapeDtypeStruct((part, words), BF16),
        in_specs=[
            pl.BlockSpec((slots, part), lambda g: (0, 0)),
            pl.BlockSpec((sources, capacity, tokens), lambda g: (jnp.maximum(g - 1, 0), 0, 0)),
            pl.BlockSpec((1, sources, tokens, part), lambda g: (jnp.maximum(g - 1, 0), 0, 0, 0)),
            pl.BlockSpec((1, slots, packed.shape[2]), lambda g: (g, 0, 0)),
            pl.BlockSpec((slots, kinds), lambda g: (g, 0)),
        ],
        out_specs=pl.BlockSpec((part, words), lambda g: (0, 0)),
        scratch_shapes=[
            pltpu.VMEM((slots, part), BF16),
            pltpu.VMEM((part, slots), BF16),
            pltpu.VMEM((part, words), F32),
        ],
        compiler_params=pltpu.CompilerParams(dimension_semantics=("arbitrary",)),
        name="weight_product",
    )(own, pick, parts, packed, only)


def body(
    hidden,
    output_weight,
    owners,
    negatives,
    negative_mask,
    target_block,
    target_word,
    log_norm,
    cotangent,
):
    tokens, width = hidden.shape
    visits = owners.shape[1]
    per_own = negatives.shape[2]
    n_vocab = lax.axis_size("vocab")
    n_dp = lax.axis_size("dp")
    me = lax.axis_index("vocab")
    my_dp = lax.axis_index("dp")
    words = output_weight.shape[1]
    capacity = max(2, tokens * visits * 4 // (3 * n_vocab))
    if n_vocab == CUBE and n_dp == LINE:
        return cube_program(
            hidden,
            output_weight,
            owners,
            negatives,
            negative_mask,
            target_block,
            target_word,
            log_norm,
            cotangent,
            n_dp,
            capacity,
        )
    slots = n_vocab * capacity
    part = width // n_dp

    facts = jnp.concatenate(
        [
            owners.T,
            negatives.reshape(tokens, -1).T,
            negative_mask.reshape(tokens, -1).T,
            target_block[None, :],
            target_word[None, :],
        ],
        axis=0,
    ).astype(BF16)
    facts = jnp.concatenate([facts, log_norm[None, :], cotangent[None, :]], axis=0)
    facts = jnp.pad(facts, ((0, -facts.shape[0] % 16), (0, 0)))
    blocks = n_dp * n_vocab

    group_rows = lax.all_gather(hidden, "vocab", axis=0, tiled=False)
    part_rows = lax.all_to_all(hidden, "dp", split_axis=1, concat_axis=0, tiled=True)
    part_rows = jnp.roll(part_rows.reshape(n_dp, tokens, part), -my_dp, axis=0)[1:]
    facts = lax.all_gather(lax.all_gather(facts, "dp", axis=0), "vocab", axis=0)
    facts = jnp.roll(facts, -my_dp, axis=1)
    part_rows = lax.all_gather(part_rows, "vocab", axis=1)
    facts = jnp.swapaxes(facts, 0, 1).reshape(blocks, -1, tokens)

    f = facts.astype(F32)
    pairs = visits * per_own
    hit = f[:, :visits, :] == me.astype(F32)
    neg = f[:, visits : visits + pairs, :]
    mask = f[:, visits + pairs : visits + 2 * pairs, :]
    base = visits + 2 * pairs
    t_block, t_word, norm, cot = (f[:, base + i, :] for i in range(4))
    named = jnp.any(hit, axis=1)
    cand = [jnp.where(hit[:, 0], t_block + 1.0, 0.0)]
    for n in range(per_own):
        value = jnp.zeros_like(t_block)
        for v in range(visits):
            i = v * per_own + n
            value = jnp.where(hit[:, v] & (mask[:, i] == 1.0), neg[:, i] + 1.0, value)
        cand.append(value)
    only = []
    for k, value in enumerate(cand):
        for earlier in cand[:k]:
            value = jnp.where(value == earlier, 0.0, value)
        only.append(value)
    upper = jnp.triu(jnp.ones((tokens, tokens), BF16), 1)
    rank = jnp.dot(named.astype(BF16), upper, preferred_element_type=F32)
    place = jnp.where(named, rank, -1.0)
    pick = (
        place[:, None, :] == jnp.arange(capacity, dtype=jnp.int32).astype(F32)[None, :, None]
    ).astype(BF16)
    attrs = jnp.stack(cand + only + [t_word, norm, cot], axis=1).astype(BF16)
    slot_facts = jnp.einsum("sct,sat->sca", pick, attrs, preferred_element_type=F32)
    kinds = per_own + 1
    all_only = slot_facts[:, :, kinds : 2 * kinds].reshape(n_dp * slots, kinds)
    mine = slot_facts[:n_vocab].reshape(slots, -1)
    my_pick = pick[:n_vocab]

    rows = jnp.einsum("sct,sth->sch", my_pick, group_rows, preferred_element_type=F32)
    rows = rows.astype(BF16).reshape(slots, width)
    scores = jnp.dot(rows, output_weight, preferred_element_type=F32)
    word_ids = jnp.arange(words, dtype=jnp.int32)[None, :]
    word_block = (word_ids // BLOCK + 1).astype(F32)
    word_in = (word_ids % BLOCK).astype(F32)
    counts = jnp.zeros((slots, words), F32)
    for k in range(kinds):
        counts = counts + jnp.where(mine[:, k : k + 1] == word_block, 1.0, 0.0)
    hot = jnp.where(
        (mine[:, 0:1] == word_block) & (mine[:, 2 * kinds : 2 * kinds + 1] == word_in), 1.0, 0.0
    )
    norm_col = mine[:, 2 * kinds + 1 : 2 * kinds + 2]
    cot_col = mine[:, 2 * kinds + 2 : 2 * kinds + 3]
    grown = jnp.where(counts > 0.0, counts * jnp.exp(scores - norm_col), 0.0)
    grad = (cot_col * (grown - hot)).astype(BF16)

    packed = []
    for k in range(kinds):
        which = mine[:, kinds + k : kinds + k + 1]
        value = jnp.zeros((slots, BLOCK), BF16)
        for b in range(BLK_DEV):
            value = jnp.where(which == b + 1.0, grad[:, b * BLOCK : (b + 1) * BLOCK], value)
        packed.append(value)
    packed = jnp.concatenate(packed, axis=1)
    back = lax.dot_general(
        grad, output_weight, (((1,), (1,)), ((), ())), preferred_element_type=F32
    ).astype(BF16)
    back = jnp.einsum(
        "sct,sch->sth", my_pick, back.reshape(n_vocab, capacity, width), preferred_element_type=F32
    ).astype(BF16)
    hidden_grad = lax.psum_scatter(
        back.reshape(n_vocab * tokens, width), "vocab", scatter_dimension=0, tiled=True
    )
    packed = jnp.roll(lax.all_gather(packed, "dp", axis=0), -my_dp, axis=0)
    own_slots = lax.dynamic_slice_in_dim(rows, my_dp * part, part, 1)
    weight_grad = weight_product(own_slots, pick[n_vocab:], part_rows, packed, all_only, words)
    return (hidden_grad, weight_grad)


def solution(mesh):
    placed = (
        P(("dp", "vocab"), None),
        P(None, "vocab"),
        P(("dp", "vocab"), None),
        P(("dp", "vocab"), None, None),
        P(("dp", "vocab"), None, None),
        P(("dp", "vocab")),
        P(("dp", "vocab")),
        P(("dp", "vocab")),
        P(("dp", "vocab")),
    )
    return jax.shard_map(
        body,
        mesh=mesh,
        in_specs=placed,
        out_specs=(P(("dp", "vocab"), None), P("dp", "vocab")),
        check_vma=False,
    )
```

```python
import jax
import jax.numpy as jnp
from jax import lax
from jax.experimental import pallas as pl
from jax.experimental.pallas import tpu as pltpu
from jax.sharding import PartitionSpec as P

BLOCK = 128
BLK_DEV = 8
F32 = jnp.float32
BF16 = jnp.bfloat16


MESH = pl.DeviceIdType.MESH
CUBE = 8
LINE = 4
PIECES = 2
TILE = 8
NT = (((1,), (1,)), ((), ()))


def rows_at(start, count):
    return pl.ds(pl.multiple_of(start, count), count)


def make_facts(own_ref, neg_ref, mask_ref, block_ref, word_ref, norm_ref, cot_ref):
    visits, tokens = own_ref.shape
    per_own = neg_ref.shape[1]
    code = jnp.where(mask_ref[...] == 1, neg_ref[...] + 1, 0).astype(F32)
    owners = own_ref[...].astype(F32)
    lines = [owners[v : v + 1, :] for v in range(visits)] + [block_ref[...].astype(F32) + 1.0]
    lines += [code[v, n : n + 1, :] for v in range(visits) for n in range(per_own)]
    lines += [ref[...].astype(F32) for ref in (word_ref, norm_ref, cot_ref)]
    count = fact_rows(visits, per_own)
    row = lax.broadcasted_iota(jnp.int32, (count, tokens), 0)
    tile = jnp.zeros((count, tokens), F32)
    for i, line in enumerate(lines):
        tile = jnp.where(row == i, jnp.broadcast_to(line, (count, tokens)), tile)
    return tile.astype(BF16)


def fact_rows(visits, per_own):
    rows = visits * (1 + per_own) + 4
    return rows + -rows % (2 * TILE)


def read_facts(facts, me, visits, per_own):
    f = facts.astype(F32)
    sources, _, tokens = f.shape
    kinds = per_own + 1
    line = lambda i: f[:, i : i + 1, :]
    hit = [jnp.where(line(v) == me.astype(F32), 1.0, 0.0) for v in range(visits)]
    named = sum(hit[1:], hit[0])
    lines = [hit[0] * line(visits)]
    for n in range(per_own):
        terms = [hit[v] * line(visits + 1 + v * per_own + n) for v in range(visits)]
        lines.append(sum(terms[1:], terms[0]))
    base = visits + 1 + visits * per_own
    lines += [named * line(base + i) for i in range(3)] + [named]
    row = lax.broadcasted_iota(jnp.int32, (sources, TILE, tokens), 1)
    cand = jnp.zeros((sources, TILE, tokens), F32)
    for i, value in enumerate(lines):
        cand = jnp.where(row == i, jnp.broadcast_to(value, cand.shape), cand)
    only = cand
    for k in range(kinds - 1):
        earlier = jnp.broadcast_to(lines[k], cand.shape)
        only = jnp.where((row > k) & (row < kinds) & (cand == earlier), 0.0, only)
    before = lax.broadcasted_iota(jnp.int32, (tokens, tokens), 0)
    after = lax.broadcasted_iota(jnp.int32, (tokens, tokens), 1)
    upper = jnp.where(before < after, 1.0, 0.0).astype(BF16)
    flat = cand.reshape(sources * TILE, tokens).astype(BF16)
    rank = jnp.dot(flat, upper, preferred_element_type=F32).reshape(cand.shape)
    place = jnp.where(cand > 0.0, rank, -1.0)
    return cand, only, place


def pick_of(place_ref, s, line, slots):
    tokens = place_ref.shape[2]
    place = place_ref[s][line : line + 1, :]
    slot = lax.broadcasted_iota(jnp.int32, (slots, tokens), 0).astype(F32)
    return jnp.where(jnp.broadcast_to(place, (slots, tokens)) == slot, 1.0, 0.0).astype(BF16)


def chip_scores(c, kinds, g, w, cols, grads, pk):
    count = pk.shape[0]
    words = w.shape[1]
    pair = 2 * BLOCK
    at = rows_at(c * count, count)
    lane = lax.broadcasted_iota(jnp.int32, (count, BLOCK), 1).astype(F32)
    pk[...] = jnp.zeros_like(pk)

    @pl.loop(0, words // pair)
    def _(j):
        words_at = rows_at(j * pair, pair)
        scores = jnp.dot(g[at, :], w[:, words_at], preferred_element_type=F32)
        col = [jnp.broadcast_to(cols[at, i : i + 1], (count, BLOCK)) for i in range(kinds + 3)]
        only = [
            jnp.broadcast_to(cols[at, TILE + i : TILE + i + 1], (count, BLOCK))
            for i in range(kinds)
        ]
        word, norm, cot = col[kinds:]
        here = jnp.where(word == lane, 1.0, 0.0)
        sides = []
        for i in range(2):
            block = (2 * j + i + 1).astype(F32)
            counts = jnp.where(col[0] == block, 1.0, 0.0)
            hot = counts * here
            for k in range(1, kinds):
                counts = counts + jnp.where(col[k] == block, 1.0, 0.0)
            score = scores[:, i * BLOCK : (i + 1) * BLOCK]
            grown = jnp.where(counts > 0.0, counts * jnp.exp(score - norm), 0.0)
            grad = cot * (grown - hot)
            for k in range(kinds):
                spot = slice(k * BLOCK, (k + 1) * BLOCK)
                pk[:, spot] = jnp.where(only[k] == block, grad, pk[:, spot])
            sides.append(grad.astype(BF16))
        grads[at, words_at] = jnp.concatenate(sides, axis=1)


def chip_back(c, count, w, grads, b):
    width = w.shape[0]
    step = min(512, width)
    at = rows_at(c * count, count)

    @pl.loop(0, width // step)
    def _(j):
        cut = rows_at(j * step, step)
        b[at, cut] = lax.dot_general(
            grads[at, :], w[cut, :], NT, preferred_element_type=F32
        ).astype(BF16)


def add_product(lhs_t, spread, acc, out=None, first=False):
    pair = 2 * BLOCK

    @pl.loop(0, acc.shape[1] // pair)
    def _(j):
        at = rows_at(j * pair, pair)
        value = jnp.dot(lhs_t[...], spread(j, at), preferred_element_type=F32)
        if not first:
            value = value + acc[:, at]
        if out is None:
            acc[:, at] = value
        else:
            out[:, at] = value.astype(BF16)


def unpack(kinds, only_cols, packed):
    def spread(j, _):
        sides = []
        for i in range(2):
            block = (2 * j + i + 1).astype(F32)
            value = None
            for k in range(kinds):
                mine = jnp.broadcast_to(only_cols[:, k : k + 1], (only_cols.shape[0], BLOCK)) == block
                term = packed(k).astype(F32)
                value = jnp.where(mine, term, 0.0 if value is None else value)
            sides.append(value.astype(BF16))
        return jnp.concatenate(sides, axis=1)

    return spread


def flip(value, m):
    bit, out = 1, value
    while bit <= m:
        if m & bit:
            out = out + bit - 2 * bit * ((value // bit) % 2)
        bit *= 2
    return out


def cube_kernel(
    n_dp,
    h_ref,
    w_ref,
    own_ref,
    neg_ref,
    mask_ref,
    block_ref,
    word_ref,
    norm_ref,
    cot_ref,
    mine_ref,
    fx_ref,
    fy_ref,
    wg_ref,
    own_in,
    neg_in,
    mask_in,
    block_in,
    word_in,
    norm_in,
    cot_in,
    w,
    g,
    b,
    sbuf,
    sums,
    own_sum,
    hx,
    hy,
    wg,
    facts,
    place,
    ship,
    cols,
    only_cols,
    grads,
    pk,
    packed,
    parts,
    near_out,
    near_in,
    lhs,
    lhs_t,
    acc,
    send,
    recv,
    local,
):
    v = lax.axis_index("vocab")
    dp = lax.axis_index("dp")
    sib, xp, yp = flip(v, 1), flip(v, 2), flip(v, 4)
    diag = flip(v, 6)
    chip, xc, yc, dc = v // 2, xp // 2, yp // 2, diag // 2
    tokens, width = h_ref.shape
    visits, per_own = neg_in.shape[:2]
    kinds = per_own + 1
    part = width // n_dp
    half = tokens // 2
    capacity = packed.shape[2]
    count = 2 * tokens
    others = [flip(v, u) for u in range(1, CUBE)]
    groups = [flip(dp, m) for m in range(n_dp)]
    far = range(2, n_dp)
    copies = []

    barrier = pltpu.get_barrier_semaphore()
    for peer in others:
        pl.semaphore_signal(barrier, inc=1, device_id={"vocab": peer}, device_id_type=MESH)
    for peer in groups[1:]:
        pl.semaphore_signal(barrier, inc=1, device_id={"dp": peer}, device_id_type=MESH)

    def push(src, dst, **where):
        i = len(copies)
        copy = pltpu.make_async_remote_copy(
            src_ref=src,
            dst_ref=dst,
            send_sem=send.at[i],
            recv_sem=recv.at[i],
            device_id=where,
            device_id_type=MESH,
        )
        copy.start()
        copies.append(copy)
        return copy

    def wait(*items):
        for copy in items:
            copy.wait_recv()

    def dev_rows(q, first=0, rows=None):
        rows = tokens if rows is None else rows
        return rows_at(q * tokens + first, rows)

    codes_in = (own_in, neg_in, mask_in, block_in, word_in, norm_in, cot_in)
    loads = []
    for i, (src, dst) in enumerate(
        zip(
            (own_ref, neg_ref, mask_ref, block_ref, word_ref, norm_ref, cot_ref),
            codes_in,
        )
    ):
        loads.append(pltpu.make_async_copy(src, dst, local.at[2 + i]))
        loads[-1].start()
    load_h = pltpu.make_async_copy(h_ref, g.at[dev_rows(v)], local.at[1])
    load_h.start()
    load_w = pltpu.make_async_copy(w_ref, w, local.at[0])
    load_w.start()

    pl.semaphore_wait(barrier, CUBE - 1 + n_dp - 1)

    low, high = pl.ds(0, half), pl.ds(half, half)
    x_low = push(h_ref.at[low], g.at[dev_rows(v, 0, half)], vocab=xp)
    y_high = push(h_ref.at[high], g.at[dev_rows(v, half, half)], vocab=yp)
    s_own = push(h_ref, g.at[dev_rows(v)], vocab=sib)
    far_in = []
    for m in far:
        columns = rows_at(groups[m] * part, part)
        far_in.append(push(h_ref.at[:, columns], parts.at[m - 2, v], dp=groups[m]))
    for load in loads:
        load.wait()
    facts[v] = make_facts(*codes_in)
    facts_in = [push(facts.at[v], facts.at[v], vocab=peer) for peer in others]
    x_high = push(h_ref.at[high], g.at[dev_rows(v, half, half)], vocab=xp)
    y_low = push(h_ref.at[low], g.at[dev_rows(v, 0, half)], vocab=yp)

    def forward(q, first, rows, **where):
        at = dev_rows(q, first, rows)
        return push(g.at[at], g.at[at], **where)

    wait(*facts_in)
    cand, only, own_place = read_facts(facts[...], v, visits, per_own)
    place[...] = own_place
    row = lax.broadcasted_iota(jnp.int32, (tokens, tokens), 0)
    lane = lax.broadcasted_iota(jnp.int32, (tokens, tokens), 1)
    eye = jnp.where(row == lane, 1.0, 0.0).astype(BF16)
    tile_row = lax.broadcasted_iota(jnp.int32, (TILE, tokens), 0)
    tile_lane = lax.broadcasted_iota(jnp.int32, (TILE, tokens), 1).astype(F32)
    for s in range(CUBE):
        both = jnp.concatenate([cand[s], only[s]], axis=0).astype(BF16)
        cols[s * tokens : (s + 1) * tokens, :] = lax.dot_general(
            eye, both, NT, preferred_element_type=F32
        )
        mine = jnp.where(tile_row == kinds, tile_lane, jnp.where(tile_row < kinds, only[s], 0.0))
        mine = jnp.concatenate([mine, jnp.zeros_like(mine)], axis=0).astype(BF16)
        ship[0, s] = lax.dot_general(
            mine, pick_of(place, s, kinds + 3, tokens), NT, preferred_element_type=F32
        ).astype(BF16)

    packs_in = {m: [] for m in range(1, n_dp)}

    def work(c, service=None):
        near_columns = rows_at(groups[1] * part, part)
        for i in range(2):
            s = 2 * c + i
            near_out[rows_at(s * capacity, capacity), :] = jnp.dot(
                pick_of(place, s, kinds + 3, capacity),
                g[dev_rows(s), near_columns],
                preferred_element_type=F32,
            ).astype(BF16)
        at = rows_at(2 * c * capacity, 2 * capacity)
        packs_in[1].append(push(near_out.at[at], near_in.at[at], dp=groups[1]))
        chip_scores(c, kinds, g, w, cols, grads, pk)
        for i in range(2):
            s = 2 * c + i
            mine = pk[i * tokens : (i + 1) * tokens, :].astype(BF16)
            packed[0, s] = jnp.dot(
                pick_of(place, s, kinds + 3, capacity), mine, preferred_element_type=F32
            ).astype(BF16)
        two = pl.ds(2 * c, 2)
        for m in reversed(range(1, n_dp)):
            packs_in[m].append(push(packed.at[0, two], packed.at[m, two], dp=groups[m]))
            packs_in[m].append(push(ship.at[0, two], ship.at[m, two], dp=groups[m]))
        if service is not None:
            service()
        chip_back(c, count, w, grads, b)

    def pair(i, q):
        return push(b.at[dev_rows(flip(q, 1))], sbuf.at[i], vocab=sib)

    load_w.wait()
    load_h.wait()
    wait(s_own)
    work(chip)
    pair_own = pair(3, v)

    wait(x_low)
    d_low = forward(xp, 0, half, vocab=yp)
    s1 = forward(xp, 0, half, vocab=sib)
    wait(y_high)
    d_high = forward(yp, half, half, vocab=xp)
    s2 = forward(yp, half, half, vocab=sib)
    wait(x_high)
    s3 = forward(xp, half, half, vocab=sib)
    wait(y_low)
    s4 = forward(yp, 0, half, vocab=sib)
    wait(s1, s3)

    far_half = max(1, len(far) // 2)
    far_low, far_high = pl.ds(0, far_half), pl.ds(far_half, len(far) - far_half)
    far_copies = []

    def far_direct():
        wait(*far_in)
        for where in (dict(vocab=xp), dict(vocab=yp), dict(vocab=sib)):
            far_copies.append(push(parts.at[:, v], parts.at[:, v], **where))

    def add_sum(i, q, first, rows, hop=None, hop_first=0):
        step = 16

        @pl.loop(0, rows // step)
        def _(k):
            at = rows_at(first + k * step, step)
            total = b[rows_at(q * tokens + first + k * step, step), :].astype(F32)
            total = total + sbuf[i, at, :].astype(F32)
            if hop is not None:
                total = total + hop[rows_at(hop_first + k * step, step), :].astype(F32)
            sums[i, at, :] = total.astype(BF16)

    back_copies = []
    from_diag = []

    def during_y():
        wait(d_low)
        from_diag.append(forward(diag, 0, half, vocab=sib))
        wait(d_high)
        from_diag.append(forward(diag, half, half, vocab=sib))
        wait(pair_x)
        add_sum(1, xp, 0, half)
        back_copies.append(push(sums.at[1, low], fx_ref.at[low], vocab=xp))

    def y_back():
        wait(pair_y)
        add_sum(2, yp, half, half)
        back_copies.append(push(sums.at[2, high], fy_ref.at[high], vocab=yp))

    work(xc, far_direct)
    pair_x = pair(1, xp)
    wait(s2, s4)
    work(yc, during_y)
    pair_y = pair(2, yp)
    wait(*from_diag)
    y_back()
    work(dc)
    pair_d = pair(0, diag)
    wait(pair_d)
    piece = half // PIECES
    to_x, to_y = [], []
    for i in range(PIECES):
        add_sum(0, diag, i * piece, piece)
        to_x.append(
            push(sums.at[0, pl.ds(i * piece, piece)], hx.at[pl.ds(i * piece, piece)], vocab=xp)
        )
        add_sum(0, diag, half + i * piece, piece)
        to_y.append(
            push(
                sums.at[0, pl.ds(half + i * piece, piece)],
                hy.at[pl.ds(i * piece, piece)],
                vocab=yp,
            )
        )

    def hops(i):
        at = pl.ds(i * piece, piece)
        wait(to_x[i])
        add_sum(2, yp, i * piece, piece, hx, i * piece)
        back_copies.append(push(sums.at[2, at], fy_ref.at[at], vocab=yp))
        at = pl.ds(half + i * piece, piece)
        wait(to_y[i])
        add_sum(1, xp, half + i * piece, piece, hy, i * piece)
        back_copies.append(push(sums.at[1, at], fx_ref.at[at], vocab=xp))

    wait(pair_own)
    step = 16

    @pl.loop(0, tokens // step)
    def _(k):
        at = rows_at(k * step, step)
        total = b[rows_at(v * tokens + k * step, step), :].astype(F32)
        own_sum[at, :] = (total + sbuf[3, at, :].astype(F32)).astype(BF16)

    keep_mine = pltpu.make_async_copy(own_sum, mine_ref, local.at[1])
    keep_mine.start()

    chunk = lhs_t.shape[1]
    own_columns = rows_at(dp * part, part)
    for i in range(CUBE * tokens // chunk):
        at = slice(i * chunk, (i + 1) * chunk)
        lhs_t[...] = g[at, own_columns].T
        add_product(lhs_t, lambda j, words_at, at=at: grads[at, words_at], acc, first=i == 0)

    wait(*far_copies)
    far_on = [
        push(parts.at[far_low, xp], parts.at[far_low, xp], vocab=yp),
        push(parts.at[far_high, yp], parts.at[far_high, yp], vocab=xp),
    ]
    far_sib = [push(parts.at[:, q], parts.at[:, q], vocab=sib) for q in (xp, yp)]

    token_lane = lax.broadcasted_iota(jnp.int32, (capacity, tokens), 1).astype(F32)

    def slot_codes(m):
        @pl.loop(0, CUBE)
        def _(s):
            only_cols[m - 1, rows_at(s * capacity, capacity), :] = lax.dot_general(
                eye[:capacity, :], ship[m, s], NT, preferred_element_type=F32
            )

    def compact(m, c):
        for i in range(2):
            s = 2 * c + i
            at = rows_at(s * capacity, capacity)
            token = only_cols[m - 1, at, kinds : kinds + 1]
            pick = jnp.where(jnp.broadcast_to(token, token_lane.shape) == token_lane, 1.0, 0.0)
            lhs[m - 2, at, :] = jnp.dot(
                pick.astype(BF16), parts[m - 2, s], preferred_element_type=F32
            ).astype(BF16)

    def other_product(m):
        lhs_t[...] = (near_in[...] if m == 1 else lhs[m - 2]).T

        def block_of(k):
            return packed[m, :, :, k * BLOCK : (k + 1) * BLOCK].reshape(CUBE * capacity, BLOCK)

        add_product(
            lhs_t,
            unpack(kinds, only_cols.at[m - 1], block_of),
            acc,
            out=wg if m == n_dp - 1 else None,
        )

    for m in far:
        wait(*packs_in[m])
        slot_codes(m)
    wait(*far_sib)
    for m in far:
        for c in (chip, xc, yc):
            compact(m, c)
    for i in range(PIECES):
        hops(i)
    wait(*packs_in[1])
    slot_codes(1)
    other_product(1)
    wait(*far_on)
    far_last = [
        push(parts.at[far_low, diag], parts.at[far_low, diag], vocab=sib),
        push(parts.at[far_high, diag], parts.at[far_high, diag], vocab=sib),
    ]
    wait(*far_last)
    for m in far:
        compact(m, dc)
        other_product(m)

    keep_wg = pltpu.make_async_copy(wg, wg_ref, local.at[0])
    keep_wg.start()
    keep_mine.wait()
    keep_wg.wait()
    wait(*back_copies)
    for copy in copies:
        copy.wait_send()


def cube_program(
    hidden, weight, owners, negatives, mask, block, word, norm, cot, n_dp, capacity
):
    tokens, width = hidden.shape
    words = weight.shape[1]
    visits, per_own = negatives.shape[1:]
    part = width // n_dp
    slots = CUBE * capacity
    group = CUBE * tokens
    kinds = per_own + 1
    hbm = pl.BlockSpec(memory_space=pl.ANY)
    v = pltpu.VMEM
    total = 96
    state = jax.ShapeDtypeStruct((tokens, width), BF16)
    terms = pl.pallas_call(
        lambda *refs: cube_kernel(n_dp, *refs),
        out_shape=(state, state, state, jax.ShapeDtypeStruct((part, words), BF16)),
        in_specs=[hbm] * 9,
        out_specs=(hbm,) * 4,
        scratch_shapes=[
            v((visits, tokens), jnp.int32),
            v((visits, per_own, tokens), jnp.int32),
            v((visits, per_own, tokens), jnp.int32),
            v((1, tokens), jnp.int32),
            v((1, tokens), jnp.int32),
            v((1, tokens), BF16),
            v((1, tokens), BF16),
            v((width, words), BF16),
            v((group, width), BF16),
            v((group, width), BF16),
            v((4, tokens, width), BF16),
            v((3, tokens, width), BF16),
            v((tokens, width), BF16),
            v((tokens // 2, width), BF16),
            v((tokens // 2, width), BF16),
            v((part, words), BF16),
            v((CUBE, fact_rows(visits, per_own), tokens), BF16),
            v((CUBE, TILE, tokens), F32),
            v((n_dp, CUBE, 2 * TILE, tokens), BF16),
            v((group, 2 * TILE), F32),
            v((n_dp - 1, slots, 2 * TILE), F32),
            v((group, words), BF16),
            v((2 * tokens, kinds * BLOCK), F32),
            v((n_dp, CUBE, capacity, kinds * BLOCK), BF16),
            v((n_dp - 2, CUBE, tokens, part), BF16),
            v((slots, part), BF16),
            v((slots, part), BF16),
            v((n_dp - 2, slots, part), BF16),
            v((part, slots), BF16),
            v((part, words), F32),
            pltpu.SemaphoreType.DMA((total,)),
            pltpu.SemaphoreType.DMA((total,)),
            pltpu.SemaphoreType.DMA((9,)),
        ],
        compiler_params=pltpu.CompilerParams(
            collective_id=0, has_side_effects=True, vmem_limit_bytes=62 * 2**20
        ),
        name="cube",
    )(
        hidden,
        weight,
        owners.T,
        jnp.transpose(negatives, (1, 2, 0)),
        jnp.transpose(mask, (1, 2, 0)),
        block[None, :],
        word[None, :],
        norm[None, :],
        cot[None, :],
    )
    return finish(*terms)


def finish_kernel(a_ref, b_ref, c_ref, wg_ref, o_ref, out_ref, a, b, c, o, wg, sems):
    pieces = 4
    rows, deep = a.shape[0] // pieces, wg.shape[0] // pieces
    loads, stores = [], []

    def start(src, dst, i):
        copy = pltpu.make_async_copy(src, dst, sems.at[i])
        copy.start()
        return copy

    cuts = [pl.ds(i * rows, rows) for i in range(pieces)]
    deep_cuts = [pl.ds(i * deep, deep) for i in range(pieces)]
    for i, at in enumerate(cuts):
        loads.append(
            [
                start(src.at[at], dst.at[at], 3 * i + k)
                for k, (src, dst) in enumerate(((a_ref, a), (b_ref, b), (c_ref, c)))
            ]
        )
    deep_loads = [
        start(wg_ref.at[at], wg.at[at], 3 * pieces + i) for i, at in enumerate(deep_cuts)
    ]
    for i, at in enumerate(cuts):
        for copy in loads[i]:
            copy.wait()
        total = a[at, :].astype(F32) + b[at, :].astype(F32) + c[at, :].astype(F32)
        o[at, :] = total.astype(BF16)
        stores.append(start(o.at[at], o_ref.at[at], 4 * pieces + i))
    for i, at in enumerate(deep_cuts):
        deep_loads[i].wait()
        stores.append(start(wg.at[at], out_ref.at[at], 5 * pieces + i))
    for copy in stores:
        copy.wait()


def finish(mine, fx, fy, weight):
    hbm = pl.BlockSpec(memory_space=pl.ANY)
    like = lambda x: jax.ShapeDtypeStruct(x.shape, x.dtype)
    v = pltpu.VMEM
    return pl.pallas_call(
        finish_kernel,
        out_shape=(like(mine), like(weight)),
        in_specs=[hbm] * 4,
        out_specs=(hbm,) * 2,
        scratch_shapes=[v(mine.shape, BF16)] * 4
        + [v(weight.shape, BF16), pltpu.SemaphoreType.DMA((24,))],
        compiler_params=pltpu.CompilerParams(vmem_limit_bytes=60 * 2**20),
        name="finish",
    )(mine, fx, fy, weight)


def weight_kernel(own_ref, pick_ref, part_ref, packed_ref, only_ref, o_ref, lhs, lhs_t, acc):
    g = pl.program_id(0)
    sources, capacity = pick_ref.shape[:2]
    kinds = only_ref.shape[1]
    pair = 2 * BLOCK

    @pl.when(g == 0)
    def _():
        lhs[...] = own_ref[...]
        acc[...] = jnp.zeros_like(acc)

    @pl.when(g > 0)
    def _():
        for s in range(sources):
            lhs[s * capacity : (s + 1) * capacity, :] = jnp.dot(
                pick_ref[s], part_ref[0, s], preferred_element_type=F32
            ).astype(BF16)

    lhs_t[...] = lhs[...].T

    @pl.loop(0, acc.shape[1] // pair, unroll=True)
    def _(j):
        sides = []
        for i in range(2):
            block = (2 * j + i + 1).astype(F32)
            value = jnp.zeros((lhs.shape[0], BLOCK), F32)
            for k in range(kinds):
                value = jnp.where(
                    only_ref[:, k : k + 1] == block,
                    packed_ref[0, :, k * BLOCK : (k + 1) * BLOCK].astype(F32),
                    value,
                )
            sides.append(value.astype(BF16))
        spread = jnp.concatenate(sides, axis=1)
        at = pl.ds(pl.multiple_of(j * pair, pair), pair)
        acc[:, at] += jnp.dot(lhs_t[...], spread, preferred_element_type=F32)

    @pl.when(g == pl.num_programs(0) - 1)
    def _():
        o_ref[...] = acc[...].astype(BF16)


def weight_product(own, pick, parts, packed, only, words):
    groups, slots = packed.shape[:2]
    _, sources, tokens, part = parts.shape
    capacity = pick.shape[1]
    kinds = only.shape[1]
    return pl.pallas_call(
        weight_kernel,
        grid=(groups,),
        out_shape=jax.ShapeDtypeStruct((part, words), BF16),
        in_specs=[
            pl.BlockSpec((slots, part), lambda g: (0, 0)),
            pl.BlockSpec((sources, capacity, tokens), lambda g: (jnp.maximum(g - 1, 0), 0, 0)),
            pl.BlockSpec((1, sources, tokens, part), lambda g: (jnp.maximum(g - 1, 0), 0, 0, 0)),
            pl.BlockSpec((1, slots, packed.shape[2]), lambda g: (g, 0, 0)),
            pl.BlockSpec((slots, kinds), lambda g: (g, 0)),
        ],
        out_specs=pl.BlockSpec((part, words), lambda g: (0, 0)),
        scratch_shapes=[
            pltpu.VMEM((slots, part), BF16),
            pltpu.VMEM((part, slots), BF16),
            pltpu.VMEM((part, words), F32),
        ],
        compiler_params=pltpu.CompilerParams(dimension_semantics=("arbitrary",)),
        name="weight_product",
    )(own, pick, parts, packed, only)


def body(
    hidden,
    output_weight,
    owners,
    negatives,
    negative_mask,
    target_block,
    target_word,
    log_norm,
    cotangent,
):
    tokens, width = hidden.shape
    visits = owners.shape[1]
    per_own = negatives.shape[2]
    n_vocab = lax.axis_size("vocab")
    n_dp = lax.axis_size("dp")
    me = lax.axis_index("vocab")
    my_dp = lax.axis_index("dp")
    words = output_weight.shape[1]
    capacity = max(2, tokens * visits * 4 // (3 * n_vocab))
    if n_vocab == CUBE and n_dp == LINE:
        return cube_program(
            hidden,
            output_weight,
            owners,
            negatives,
            negative_mask,
            target_block,
            target_word,
            log_norm,
            cotangent,
            n_dp,
            capacity,
        )
    slots = n_vocab * capacity
    part = width // n_dp

    facts = jnp.concatenate(
        [
            owners.T,
            negatives.reshape(tokens, -1).T,
            negative_mask.reshape(tokens, -1).T,
            target_block[None, :],
            target_word[None, :],
        ],
        axis=0,
    ).astype(BF16)
    facts = jnp.concatenate([facts, log_norm[None, :], cotangent[None, :]], axis=0)
    facts = jnp.pad(facts, ((0, -facts.shape[0] % 16), (0, 0)))
    blocks = n_dp * n_vocab

    group_rows = lax.all_gather(hidden, "vocab", axis=0, tiled=False)
    part_rows = lax.all_to_all(hidden, "dp", split_axis=1, concat_axis=0, tiled=True)
    part_rows = jnp.roll(part_rows.reshape(n_dp, tokens, part), -my_dp, axis=0)[1:]
    facts = lax.all_gather(lax.all_gather(facts, "dp", axis=0), "vocab", axis=0)
    facts = jnp.roll(facts, -my_dp, axis=1)
    part_rows = lax.all_gather(part_rows, "vocab", axis=1)
    facts = jnp.swapaxes(facts, 0, 1).reshape(blocks, -1, tokens)

    f = facts.astype(F32)
    pairs = visits * per_own
    hit = f[:, :visits, :] == me.astype(F32)
    neg = f[:, visits : visits + pairs, :]
    mask = f[:, visits + pairs : visits + 2 * pairs, :]
    base = visits + 2 * pairs
    t_block, t_word, norm, cot = (f[:, base + i, :] for i in range(4))
    named = jnp.any(hit, axis=1)
    cand = [jnp.where(hit[:, 0], t_block + 1.0, 0.0)]
    for n in range(per_own):
        value = jnp.zeros_like(t_block)
        for v in range(visits):
            i = v * per_own + n
            value = jnp.where(hit[:, v] & (mask[:, i] == 1.0), neg[:, i] + 1.0, value)
        cand.append(value)
    only = []
    for k, value in enumerate(cand):
        for earlier in cand[:k]:
            value = jnp.where(value == earlier, 0.0, value)
        only.append(value)
    upper = jnp.triu(jnp.ones((tokens, tokens), BF16), 1)
    rank = jnp.dot(named.astype(BF16), upper, preferred_element_type=F32)
    place = jnp.where(named, rank, -1.0)
    pick = (
        place[:, None, :] == jnp.arange(capacity, dtype=jnp.int32).astype(F32)[None, :, None]
    ).astype(BF16)
    attrs = jnp.stack(cand + only + [t_word, norm, cot], axis=1).astype(BF16)
    slot_facts = jnp.einsum("sct,sat->sca", pick, attrs, preferred_element_type=F32)
    kinds = per_own + 1
    all_only = slot_facts[:, :, kinds : 2 * kinds].reshape(n_dp * slots, kinds)
    mine = slot_facts[:n_vocab].reshape(slots, -1)
    my_pick = pick[:n_vocab]

    rows = jnp.einsum("sct,sth->sch", my_pick, group_rows, preferred_element_type=F32)
    rows = rows.astype(BF16).reshape(slots, width)
    scores = jnp.dot(rows, output_weight, preferred_element_type=F32)
    word_ids = jnp.arange(words, dtype=jnp.int32)[None, :]
    word_block = (word_ids // BLOCK + 1).astype(F32)
    word_in = (word_ids % BLOCK).astype(F32)
    counts = jnp.zeros((slots, words), F32)
    for k in range(kinds):
        counts = counts + jnp.where(mine[:, k : k + 1] == word_block, 1.0, 0.0)
    hot = jnp.where(
        (mine[:, 0:1] == word_block) & (mine[:, 2 * kinds : 2 * kinds + 1] == word_in), 1.0, 0.0
    )
    norm_col = mine[:, 2 * kinds + 1 : 2 * kinds + 2]
    cot_col = mine[:, 2 * kinds + 2 : 2 * kinds + 3]
    grown = jnp.where(counts > 0.0, counts * jnp.exp(scores - norm_col), 0.0)
    grad = (cot_col * (grown - hot)).astype(BF16)

    packed = []
    for k in range(kinds):
        which = mine[:, kinds + k : kinds + k + 1]
        value = jnp.zeros((slots, BLOCK), BF16)
        for b in range(BLK_DEV):
            value = jnp.where(which == b + 1.0, grad[:, b * BLOCK : (b + 1) * BLOCK], value)
        packed.append(value)
    packed = jnp.concatenate(packed, axis=1)
    back = lax.dot_general(
        grad, output_weight, (((1,), (1,)), ((), ())), preferred_element_type=F32
    ).astype(BF16)
    back = jnp.einsum(
        "sct,sch->sth", my_pick, back.reshape(n_vocab, capacity, width), preferred_element_type=F32
    ).astype(BF16)
    hidden_grad = lax.psum_scatter(
        back.reshape(n_vocab * tokens, width), "vocab", scatter_dimension=0, tiled=True
    )
    packed = jnp.roll(lax.all_gather(packed, "dp", axis=0), -my_dp, axis=0)
    own_slots = lax.dynamic_slice_in_dim(rows, my_dp * part, part, 1)
    weight_grad = weight_product(own_slots, pick[n_vocab:], part_rows, packed, all_only, words)
    return (hidden_grad, weight_grad)


def solution(mesh):
    placed = (
        P(("dp", "vocab"), None),
        P(None, "vocab"),
        P(("dp", "vocab"), None),
        P(("dp", "vocab"), None, None),
        P(("dp", "vocab"), None, None),
        P(("dp", "vocab")),
        P(("dp", "vocab")),
        P(("dp", "vocab")),
        P(("dp", "vocab")),
    )
    return jax.shard_map(
        body,
        mesh=mesh,
        in_specs=placed,
        out_specs=(P(("dp", "vocab"), None), P("dp", "vocab")),
        check_vma=False,
    )
```
